768 devices in a mesh: seq: 48 (over x, z), tp: 16 (over y, core).
Axes of the slice: x: 4, y: 8, z: 12, core: 2. Of those that a mesh axis runs over, the one named last changes fastest.
Arguments:
- tokens: bfloat16 [12288, 4096], P('seq', 'tp'), may hold values from -6 to 6
- w_qkv: bfloat16 [3, 4096, 4096], P(None, None, 'tp'), may hold values from -0.09375 to 0.09375
- forget: float32 [12288, 32], P('seq', 'tp'), as said below
- out_grad: bfloat16 [12288, 4096], P('seq', 'tp'), may hold values from -6 to 6
- doc_lengths: int32 [16], replicated, may hold values from 1 to 6144, 12288 in all
Outputs:
- attn_out: float32 [12288, 4096], P('seq', 'tp')
- input_grad: float32 [12288, 4096], P('seq', 'tp')
The draws below stay inside these ranges and needn't reach their ends.
Inputs may be any that keep to these rules, and one draw needn't show every extreme that they name: `doc_lengths`: the documents' lengths in stream order; they sum to 12288, and the longest has exactly 6144 tokens. `forget`: log decay factors, all negative.
All inputs are finite; a program needn't handle non-finite values.
Results may differ from the reference program's by a relative error of at most 0.0046.
Values may be sent and summed in bfloat16 or wider, within the bound.
A program may use at most 64 MiB of HBM per device.

```python
import math
import jax
import jax.numpy as jnp
import numpy as np
from jax import lax

D = 4096
ATTN_GROUPINGS = 32
DH = 128
TOK_DEV = 256
DOCS = 16
PACKED_LENGTH = 12288
MOST = 6144
BLOCK = 256


def draw_forget(key, part):
    sampling_rng_keys = jax.random.split(key, 7)
    fast_share = 0.5
    fast_heads = jax.random.uniform(sampling_rng_keys[0], (ATTN_GROUPINGS,)) < fast_share
    fast_rate = jnp.exp(jax.random.uniform(sampling_rng_keys[1], (ATTN_GROUPINGS,), minval=math.log(1.0 / 50.0), maxval=math.log(1.0 / 30.0)))
    slow_rate = jnp.exp(jax.random.uniform(sampling_rng_keys[2], (ATTN_GROUPINGS,), minval=math.log(0.05), maxval=math.log(0.4))) / PACKED_LENGTH
    forgetting_rate_param = jnp.where(fast_heads, fast_rate, slow_rate)
    segment_multiplier = jnp.exp(jax.random.uniform(sampling_rng_keys[3], (PACKED_LENGTH // TOK_DEV, 1), minval=math.log(0.5), maxval=0.0))
    segment_multiplier = jnp.repeat(segment_multiplier, TOK_DEV, axis=0)
    position_multiplier = jnp.exp(jax.random.uniform(sampling_rng_keys[4], (PACKED_LENGTH, ATTN_GROUPINGS), minval=-math.log(2.0), maxval=math.log(2.0)))
    document_spans = jax.random.uniform(sampling_rng_keys[5], (PACKED_LENGTH, ATTN_GROUPINGS)) < 2.0 / PACKED_LENGTH
    kept_fraction = jax.random.uniform(sampling_rng_keys[6], (PACKED_LENGTH, ATTN_GROUPINGS), minval=0.6, maxval=0.8)
    payload_vectors = -forgetting_rate_param[None, :] * segment_multiplier * position_multiplier + jnp.where(document_spans, jnp.log(kept_fraction), 0.0)
    return payload_vectors.astype(jnp.float32)


def steps_of(own_key, dims, pieces, smallest, top_value):
    def one(axis_at, parts):
        draws = jax.random.uniform(jax.random.fold_in(jax.random.fold_in(own_key, 6), axis_at), (parts,), jnp.float32, smallest / len(pieces), top_value / len(pieces))
        return jnp.repeat(jnp.exp(draws), dims[axis_at] // parts).reshape((-1,) + (1,) * (len(dims) - axis_at - 1))

    gain = one(*pieces[0])
    for cut in pieces[1:]:
        gain = gain * one(*cut)
    return gain


def profile(number_of, total, bound, skew):
    portions = [(1 << 20) // math.isqrt(rank ** skew) + 1 for rank in range(2, number_of + 1)]
    spare, counts = total - bound - (number_of - 1), [1] * (number_of - 1)
    while spare > 0:
        candidates = [i for i in range(number_of - 1) if counts[i] < bound]
        mass, budget = sum([portions[i] for i in candidates]), spare
        for i in candidates:
            extra = min(bound - counts[i], max(1, budget * portions[i] // mass), spare)
            counts[i] = counts[i] + extra
            spare = spare - extra
    return np.array([bound] + counts)


def ragged_sizes(stream_key, count, total, most, slope):
    if count == 2:
        one = jax.random.randint(stream_key, (), max(1, total - most), min(most, total - 1) + 1)
        return jnp.stack([one, total - one])
    sizes = jnp.asarray(profile(count, total, most, slope), jnp.int32)
    twos = (count - 1) // 2
    donor, sink = sizes[1:1 + 2 * twos:2], sizes[2:2 + 2 * twos:2]
    slack = jnp.minimum(donor - 1, most - sink)
    passed = jax.random.randint(jax.random.fold_in(stream_key, 1), (twos,), 0, 1 << 20) % (slack + 1)
    sizes = sizes.at[1:1 + 2 * twos:2].set(donor - passed).at[2:2 + 2 * twos:2].set(sink + passed)
    return sizes[jax.random.permutation(jax.random.fold_in(stream_key, 2), count)]


def gaussian(stream_key, shape, deviation, reach, shards=(), held_as=jnp.bfloat16):
    result = deviation * jax.random.normal(stream_key, shape, jnp.float32)
    if shards:
        result = result * steps_of(stream_key, shape, shards, -0.22, 0.18)
    return jnp.clip(result, -reach, reach).astype(held_as)


def setup_inputs(seed: int = 0) -> dict:
    streams_of = jax.random.split(jax.random.key(seed), 6)
    tokens = gaussian(streams_of[0], (PACKED_LENGTH, D), 1.0, 6.0, ((0, 48), (1, 16)))
    w_qkv = gaussian(streams_of[1], (3, D, ATTN_GROUPINGS * DH), D ** -0.5, 0.09375, ((2, 16),))
    forget = draw_forget(jax.random.fold_in(streams_of[5], 71), 0)
    out_grad = gaussian(streams_of[3], (PACKED_LENGTH, ATTN_GROUPINGS * DH), 1.0, 6.0, ((0, 48), (1, 16)))
    doc_lengths = ragged_sizes(streams_of[4], DOCS, PACKED_LENGTH, MOST, 2).astype(jnp.int32)
    return {"tokens": tokens, "w_qkv": w_qkv, "forget": forget, "out_grad": out_grad, "doc_lengths": doc_lengths}


HIGHEST = lax.Precision.HIGHEST

def document_ids(doc_lengths, positions):
    doc_ends = jnp.cumsum(doc_lengths).astype(jnp.int32)
    return lax.optimization_barrier(jnp.sum((positions[:, None] >= doc_ends[None, :]).astype(jnp.int32), axis=1)).astype(jnp.int32)

def head_forward(query_rows, key_rows, value_rows, log_decay, doc_ids):
    block_count = PACKED_LENGTH // BLOCK
    block_docs = doc_ids.reshape(block_count, BLOCK)
    prior_docs = jnp.concatenate([jnp.full((1,), -1, jnp.int32), block_docs[:-1, -1]]).astype(jnp.int32)
    lower = jnp.tril(jnp.ones((BLOCK, BLOCK), jnp.bool_))

    def advance(state_in, block_items):
        query_blk, key_blk, value_blk, decay_blk, docs_blk, prior_doc = block_items
        cumulative = jnp.cumsum(decay_blk)
        carried = docs_blk == prior_doc
        same_doc = (docs_blk[:, None] == docs_blk[None, :]) & lower
        log_gap = jnp.where(same_doc, cumulative[:, None] - cumulative[None, :], 0.0)
        weights = jnp.where(same_doc, jnp.exp(log_gap), 0.0)
        scores = jnp.dot(query_blk, key_blk.T, precision=HIGHEST) * weights
        intra_out = jnp.dot(scores, value_blk, precision=HIGHEST)
        lead_weight = jnp.where(carried, jnp.exp(cumulative), 0.0)
        inter_out = lead_weight[:, None] * jnp.dot(query_blk, state_in, precision=HIGHEST)
        tail_weight = jnp.where(docs_blk == docs_blk[-1], jnp.exp(cumulative[-1] - cumulative), 0.0)
        keep_state = jnp.where(carried[-1], jnp.exp(cumulative[-1]), 0.0)
        state_out = keep_state * state_in + jnp.dot((key_blk * tail_weight[:, None]).T, value_blk, precision=HIGHEST)
        return (state_out, (intra_out + inter_out) / DH)
    zero_state = jnp.zeros((DH, DH), jnp.float32)
    block_items = (query_rows.reshape(block_count, BLOCK, DH), key_rows.reshape(block_count, BLOCK, DH), value_rows.reshape(block_count, BLOCK, DH), log_decay.reshape(block_count, BLOCK), block_docs, prior_docs)
    outputs = lax.scan(advance, zero_state, block_items)[1]
    return outputs.reshape(PACKED_LENGTH, DH)

def reference(tokens, w_qkv, forget, out_grad, doc_lengths):
    positions = jnp.arange(PACKED_LENGTH, dtype=jnp.int32)
    doc_ids = document_ids(doc_lengths, positions)
    projected = [jnp.dot(tokens, w_qkv[proj_index], preferred_element_type=jnp.float32).astype(jnp.bfloat16) for proj_index in range(3)]

    def per_head(matrix):
        return matrix.astype(jnp.float32).reshape(PACKED_LENGTH, ATTN_GROUPINGS, DH).transpose(1, 0, 2)

    def head_pass(head_items):
        query_rows, key_rows, value_rows, log_decay, grad_rows = head_items

        def forward(query_in, key_in, value_in):
            return head_forward(query_in, key_in, value_in, log_decay, doc_ids)
        outputs, pullback = jax.vjp(forward, query_rows, key_rows, value_rows)
        grad_query, grad_key, grad_value = pullback(grad_rows)
        return (outputs, grad_query, grad_key, grad_value)
    outputs, grad_query, grad_key, grad_value = lax.map(head_pass, (per_head(projected[0]), per_head(projected[1]), per_head(projected[2]), forget.T, per_head(out_grad)))

    def merge_heads(stack):
        return stack.transpose(1, 0, 2).reshape(PACKED_LENGTH, ATTN_GROUPINGS * DH)
    grads_merged = [merge_heads(grad_stack).astype(jnp.bfloat16) for grad_stack in (grad_query, grad_key, grad_value)]
    attn_out = merge_heads(outputs).astype(jnp.float32)
    grad_terms = jnp.zeros((PACKED_LENGTH, D), jnp.float32)
    for proj_index in range(3):
        grad_terms = grad_terms + jnp.dot(grads_merged[proj_index], w_qkv[proj_index].T, preferred_element_type=jnp.float32)
    return (attn_out, grad_terms)
```

```python
import functools

import jax
import jax.numpy as jnp
from jax import lax
from jax.experimental import pallas as pl
from jax.experimental.pallas import tpu as pltpu
from jax.sharding import PartitionSpec as P

DH = 128
F32 = jnp.float32
BF16 = jnp.bfloat16
MESH = pl.DeviceIdType.MESH


def dot_nn(a, b):
    return lax.dot_general(a, b, (((1,), (0,)), ((), ())), preferred_element_type=F32)


def dot_nt(a, b):
    return lax.dot_general(a, b, (((1,), (1,)), ((), ())), preferred_element_type=F32)


def dot_tn(a, b):
    return lax.dot_general(a, b, (((0,), (0,)), ((), ())), preferred_element_type=F32)


def kernel(
    X, Z, Y, R, C, SR, docs,
    tokens, w, forget, out_grad, doc_lengths,
    attn_out, input_grad,
    wv, tok, fg, og, acc, gr, attn, fin,
    weight, lead, tail, part,
    lzs, lz, lxs, lx, coef, cum, pre,
    st, rc, ts, tx, bk, rt,
    sbs, sbr, own, rsend, rrecv, lsend, lrecv,
    ld_sem,
    agr_s, agr_r, agl_s, agl_r, sib_s, sib_r,
    e1_s, e1_r, e2_s, e2_r, pa_s, pa_r, pb_s, pb_r, pc_s, pc_r,
    rsib_s, rsib_r, rsr_s, rsr_r, rsl_s, rsl_r,
):
    heads = C // DH
    half = R // 2
    hops = Y // 2
    msgs = 2 * hops - 1
    seq = lax.axis_index("seq")
    tp = lax.axis_index("tp")
    x = lax.div(seq, Z)
    z = lax.rem(seq, Z)
    y = lax.div(tp, 2)
    c = lax.rem(tp, 2)

    def chip(o):
        return lax.rem(y + (o + Y), Y)

    right = (seq, chip(1) * 2 + c)
    left = (seq, chip(-1) * 2 + c)
    sibling = (seq, y * 2 + (1 - c))

    def zat(dz):
        return lax.rem(z + dz, Z)

    def xat(dx):
        return lax.rem(x + dx, X)

    def zpeer(dz):
        return (x * Z + zat(dz), tp)

    def xpeer(dx):
        return (xat(dx) * Z + z, tp)

    def remote(src, dst, ssem, rsem, dev):
        return pltpu.make_async_remote_copy(
            src_ref=src, dst_ref=dst, send_sem=ssem, recv_sem=rsem,
            device_id=dev, device_id_type=MESH,
        )

    own_tok = tok.at[tp]
    ld_tok = pltpu.make_async_copy(tokens, own_tok, ld_sem.at[0])
    ld_fg = pltpu.make_async_copy(forget, fg, ld_sem.at[1])
    ld_w = pltpu.make_async_copy(w, wv, ld_sem.at[2])
    ld_og = pltpu.make_async_copy(out_grad, og, ld_sem.at[3])
    ld_tok.start()
    ld_fg.start()
    ld_w.start()
    ld_og.start()

    barrier = pltpu.get_barrier_semaphore()
    peers = [right, left, sibling]
    peers += [zpeer(dz) for dz in range(1, Z)]
    peers += [xpeer(dx) for dx in range(1, X)]
    for dev in peers:
        pl.semaphore_signal(barrier, inc=1, device_id=dev, device_id_type=MESH)
    pl.semaphore_wait(barrier, len(peers))

    def half_of(ref, h):
        return ref.at[pl.ds(h * half, half)]

    def r_half(i):
        return i % 2

    def l_half(i):
        return 1 - i % 2

    def r_place(i):
        return half_of(tok.at[chip(-(i // 2)) * 2 + c], r_half(i))

    def l_place(i):
        return half_of(tok.at[chip(i // 2) * 2 + c], l_half(i))

    ag_r = [remote(r_place(i), r_place(i), agr_s.at[i], agr_r.at[i], right) for i in range(msgs)]
    ag_l = [remote(l_place(i), l_place(i), agl_s.at[i], agl_r.at[i], left) for i in range(msgs)]

    def r_landed(i):
        return half_of(tok.at[chip(-(i // 2) - 1) * 2 + c], r_half(i))

    def l_landed(i):
        return half_of(tok.at[chip(i // 2 + 1) * 2 + c], l_half(i))

    def sib_place(k, core):
        if k == 0:
            return tok.at[y * 2 + core]
        if k <= msgs:
            i = k - 1
            return half_of(tok.at[chip(-(i // 2) - 1) * 2 + core], r_half(i))
        i = k - 1 - msgs
        return half_of(tok.at[chip(i // 2 + 1) * 2 + core], l_half(i))

    sib_out = [
        remote(sib_place(k, c), sib_place(k, c), sib_s.at[k], sib_r.at[k], sibling)
        for k in range(2 * msgs + 1)
    ]
    sib_in = [
        remote(sib_place(k, 1 - c), sib_place(k, 1 - c), sib_s.at[k], sib_r.at[k], sibling)
        for k in range(2 * msgs + 1)
    ]
    in_r = [remote(r_landed(i), r_landed(i), agr_s.at[i], agr_r.at[i], right) for i in range(msgs)]
    in_l = [remote(l_landed(i), l_landed(i), agl_s.at[i], agl_r.at[i], left) for i in range(msgs)]

    ld_tok.wait()
    for i in range(2):
        ag_r[i].start()
        ag_l[i].start()
    sib_out[0].start()

    ld_fg.wait()
    ends = []
    total = jnp.int32(0)
    for j in range(docs):
        total = total + doc_lengths[j]
        ends.append(total)
    offset = seq * R

    def doc_of(position):
        count = jnp.int32(0)
        for e in ends:
            count = count + jnp.where(position >= e, 1, 0).astype(jnp.int32)
        return count

    prior = jnp.where(offset > 0, doc_of(offset - 1), -1)
    last = doc_of(offset + R - 1)
    doc_row = doc_of(offset + lax.broadcasted_iota(jnp.int32, (1, R), 1))
    doc_col = doc_of(offset + lax.broadcasted_iota(jnp.int32, (R, 1), 0))
    rows = lax.broadcasted_iota(jnp.int32, (R, R), 0)
    cols = lax.broadcasted_iota(jnp.int32, (R, R), 1)
    mask = (doc_col == doc_row) & (rows >= cols)
    lane = (R, DH)
    totals = []
    for h in range(heads):
        fcol = jnp.broadcast_to(fg[:, h : h + 1], (R, R))
        lrow = jnp.sum(jnp.where(rows <= cols, fcol, 0.0), axis=0, keepdims=True)
        lcol = jnp.sum(jnp.where(rows == cols, lrow, 0.0), axis=1, keepdims=True)
        gap = jnp.where(mask, lcol - lrow, 0.0)
        weight[h] = jnp.where(mask, jnp.exp(gap), 0.0)
        ltot = lrow[:, R - 1 : R]
        totals.append(ltot)
        lead[h] = jnp.broadcast_to(jnp.where(doc_col == prior, jnp.exp(lcol), 0.0), lane)
        tail[h] = jnp.broadcast_to(jnp.where(doc_col == last, jnp.exp(ltot - lcol), 0.0), lane)
    row8 = lax.broadcasted_iota(jnp.int32, (8, DH), 0)
    lzs[...] = jnp.where(row8 == 0, totals[0], totals[1])
    lz[z] = lzs[...]
    e1 = [
        remote(lzs, lz.at[z], e1_s.at[dz - 1], e1_r.at[dz - 1], zpeer(dz)) for dz in range(1, Z)
    ]
    for cp in e1:
        cp.start()

    srow = lax.broadcasted_iota(jnp.int32, (SR, DH), 0) + z * SR
    is_back = srow >= heads * DH
    second = (lax.rem(srow, 2 * DH)) >= DH

    def decays():
        for dz in range(1, Z):
            src = lax.rem(z + (Z - dz), Z)
            remote(lzs, lz.at[src], e1_s.at[dz - 1], e1_r.at[dz - 1], zpeer(dz)).wait_recv()
        place = x * Z + lax.broadcasted_iota(jnp.int32, (16, DH), 0)
        through = place > 0
        for e in ends:
            through = through & jnp.logical_not((e >= place * R) & (e < place * R + R))
        thru = jnp.where(through, 1.0, 0.0)
        a = []
        for p in range(Z):
            v = lz[p]
            a.append([jnp.where(thru[p : p + 1] > 0, jnp.exp(v[h : h + 1]), 0.0) for h in range(heads)])
        up = [jnp.ones((1, DH), F32)] * heads
        for p in range(Z):
            coef[p] = jnp.where(second, a[p][1], a[p][0])
            cum[p] = jnp.where(second, up[1], up[0])
            up = [up[h] * a[p][h] for h in range(heads)]
        down = [jnp.ones((1, DH), F32)] * heads
        for p in reversed(range(Z)):
            cum[p] = jnp.where(is_back, jnp.where(second, down[1], down[0]), cum[p])
            down = [down[h] * a[p][h] for h in range(heads)]
        lxs[...] = jnp.where(row8 == 0, up[0], up[1])
        lx[x] = lxs[...]
        for dx in range(1, X):
            remote(lxs, lx.at[x], e2_s.at[dx - 1], e2_r.at[dx - 1], xpeer(dx)).start()

    def project(offsets, m):
        out = None
        for o in offsets:
            for core in range(2):
                j = chip(o) * 2 + core
                term = dot_nn(tok[j], wv[m, pl.ds(pl.multiple_of(j * C, C), C), :])
                out = term if out is None else out + term
        return out

    def project_hop(k):
        offsets = [0] if k == 0 else [-k, k]
        for m in range(3):
            if k == 0:
                acc[m] = project(offsets, m)
            else:
                acc[m] += project(offsets, m)

    def sib_wait(k):
        if k == 0:
            sib_in[0].wait_recv()
            return
        for i in (2 * k - 2, 2 * k - 1):
            if i < msgs:
                sib_in[1 + i].wait_recv()
                sib_in[1 + msgs + i].wait_recv()

    for k in range(1, hops + 1):
        for i in (2 * k - 2, 2 * k - 1):
            if i < msgs:
                in_r[i].wait_recv()
                if i + 2 < msgs:
                    ag_r[i + 2].start()
                sib_out[1 + i].start()
                in_l[i].wait_recv()
                if i + 2 < msgs:
                    ag_l[i + 2].start()
                sib_out[1 + msgs + i].start()
        if k == 1:
            ld_w.wait()
            ld_og.wait()
        if k == 2:
            decays()
        sib_wait(k - 1)
        project_hop(k - 1)

    sib_wait(hops)
    for m in range(3):
        acc[m] += project([hops], m)

    def head(m, h):
        return acc[m, :, pl.ds(h * DH, DH)].astype(BF16)

    def grad_head(h):
        return og[:, pl.ds(h * DH, DH)]

    for h in range(heads):
        kt = (head(1, h).astype(F32) * tail[h]).astype(BF16)
        st[pl.ds(h * DH, DH), :] = dot_tn(kt, head(2, h)).astype(BF16)
        ql = (head(0, h).astype(F32) * lead[h]).astype(BF16)
        st[pl.ds((heads + h) * DH, DH), :] = (
            dot_tn(ql, grad_head(h)) * (1.0 / DH)
        ).astype(BF16)
    if Z * SR > 2 * heads * DH:
        spare = Z * SR - 2 * heads * DH
        st[pl.ds(2 * heads * DH, spare), :] = jnp.zeros((spare, DH), BF16)

    def sliced(ref, p):
        return ref.at[pl.ds(pl.multiple_of(p * SR, SR), SR)]

    for dz in range(1, Z):
        remote(
            sliced(st, zat(dz)), rc.at[z], pa_s.at[dz - 1], pa_r.at[dz - 1], zpeer(dz)
        ).start()
    rc[z] = st[pl.ds(pl.multiple_of(z * SR, SR), SR), :]

    def inside(h):
        q, k, v, g = head(0, h), head(1, h), head(2, h), grad_head(h)
        cols_h = pl.ds(h * DH, DH)
        a = (dot_nt(q, k) * weight[h]).astype(BF16)
        b = (dot_nt(g, v) * weight[h]).astype(BF16)
        part[0, :, cols_h] = dot_nn(a, v)
        part[1, :, cols_h] = dot_nn(b, k)
        part[2, :, cols_h] = dot_tn(b, q)
        part[3, :, cols_h] = dot_tn(a, g)

    inside(0)

    for dz in range(1, Z):
        src = lax.rem(z + (Z - dz), Z)
        remote(
            sliced(st, src), rc.at[src], pa_s.at[dz - 1], pa_r.at[dz - 1], zpeer(dz)
        ).wait_recv()
    run = jnp.zeros((SR, DH), F32)
    for p in range(Z):
        pre[p] = run
        run = coef[p] * run + rc[p].astype(F32)
    back = jnp.zeros((SR, DH), F32)
    for p in reversed(range(Z)):
        pre[p] = jnp.where(is_back, back, pre[p])
        back = coef[p] * back + rc[p].astype(F32)
    ts[...] = jnp.where(is_back, back, run).astype(BF16)
    tx[x] = ts[...]
    for dx in range(1, X):
        remote(ts, tx.at[x], pb_s.at[dx - 1], pb_r.at[dx - 1], xpeer(dx)).start()

    inside(1)

    for dx in range(1, X):
        src = lax.rem(x + (X - dx), X)
        remote(lxs, lx.at[src], e2_s.at[dx - 1], e2_r.at[dx - 1], xpeer(dx)).wait_recv()
        remote(ts, tx.at[src], pb_s.at[dx - 1], pb_r.at[dx - 1], xpeer(dx)).wait_recv()
    run = jnp.zeros((SR, DH), F32)
    back = jnp.zeros((SR, DH), F32)
    for p in range(X):
        v = lx[p]
        line = jnp.where(second, v[1:2], v[0:1])
        run = jnp.where(x > p, line * run + tx[p].astype(F32), run)
    for p in reversed(range(X)):
        v = lx[p]
        line = jnp.where(second, v[1:2], v[0:1])
        back = jnp.where(x < p, line * back + tx[p].astype(F32), back)
    carry = jnp.where(is_back, back, run)
    for p in range(Z):
        bk[p] = (pre[p] + cum[p] * carry).astype(BF16)
    for dz in range(1, Z):
        remote(
            bk.at[zat(dz)], sliced(rt, z), pc_s.at[dz - 1], pc_r.at[dz - 1], zpeer(dz)
        ).start()
    rt[pl.ds(pl.multiple_of(z * SR, SR), SR), :] = bk[z]

    for cp in ag_r + ag_l + sib_out + e1:
        cp.wait_send()
    for dx in range(1, X):
        remote(lxs, lx.at[x], e2_s.at[dx - 1], e2_r.at[dx - 1], xpeer(dx)).wait_send()
        remote(ts, tx.at[x], pb_s.at[dx - 1], pb_r.at[dx - 1], xpeer(dx)).wait_send()
    for dz in range(1, Z):
        remote(
            sliced(st, zat(dz)), rc.at[z], pa_s.at[dz - 1], pa_r.at[dz - 1], zpeer(dz)
        ).wait_send()

    for dz in range(1, Z):
        src = lax.rem(z + (Z - dz), Z)
        remote(
            bk.at[src], sliced(rt, src), pc_s.at[dz - 1], pc_r.at[dz - 1], zpeer(dz)
        ).wait_recv()

    scale = 1.0 / DH
    for h in range(heads):
        q, k, v, g = head(0, h), head(1, h), head(2, h), grad_head(h)
        cols_h = pl.ds(h * DH, DH)
        state = rt[pl.ds(h * DH, DH), :]
        after = rt[pl.ds((heads + h) * DH, DH), :]
        gr[0, :, cols_h] = (
            (part[1, :, cols_h] + lead[h] * dot_nt(g, state)) * scale
        ).astype(BF16)
        gr[1, :, cols_h] = (
            part[2, :, cols_h] * scale + tail[h] * dot_nt(v, after)
        ).astype(BF16)
        gr[2, :, cols_h] = (
            part[3, :, cols_h] * scale + tail[h] * dot_nn(k, after)
        ).astype(BF16)
        attn[:, cols_h] = (part[0, :, cols_h] + lead[h] * dot_nn(q, state)) * scale
    st_attn = pltpu.make_async_copy(attn, attn_out, ld_sem.at[4])
    st_attn.start()

    order = [hops]
    for k in reversed(range(1, hops)):
        order += [k, -k]
    order.append(0)
    slot = {o: i for i, o in enumerate(order)}
    slot[-hops] = slot[hops]

    def share(j):
        out = None
        for m in range(3):
            term = dot_nt(gr[m], wv[m, pl.ds(pl.multiple_of(j * C, C), C), :])
            out = term if out is None else out + term
        return out

    def rsib(s):
        return remote(sbs.at[s], sbr.at[s], rsib_s.at[s], rsib_r.at[s], sibling)

    def shares(o):
        s = slot[o]
        sbs[s] = share(chip(o) * 2 + (1 - c)).astype(BF16)
        rsib(s).start()
        own[s] = share(chip(o) * 2 + c)

    joined = set()

    def both(o, h):
        s = slot[o]
        if s not in joined:
            rsib(s).wait_recv()
            joined.add(s)
        part_rows = pl.ds(h * half, half)
        return own[s, part_rows, :] + sbr[s, part_rows, :].astype(F32)

    def rs_r(i):
        return remote(rsend.at[i], rrecv.at[i], rsr_s.at[i], rsr_r.at[i], right)

    def rs_l(i):
        return remote(lsend.at[i], lrecv.at[i], rsl_s.at[i], rsl_r.at[i], left)

    def step(i):
        o = hops if i == 0 else hops - 1 - (i - 1) // 2
        h = i % 2
        value = both(o, h)
        if i >= 2:
            rs_r(i - 2).wait_recv()
            value = value + rrecv[i - 2].astype(F32)
        rsend[i] = value.astype(BF16)
        rs_r(i).start()
        value = both(-o, 1 - h)
        if i >= 2:
            rs_l(i - 2).wait_recv()
            value = value + lrecv[i - 2].astype(F32)
        lsend[i] = value.astype(BF16)
        rs_l(i).start()

    shares(hops)
    done = 0
    for k in reversed(range(1, hops)):
        shares(k)
        shares(-k)
        if k == hops - 1:
            step(0)
            step(1)
            done = 2
        else:
            step(done)
            done += 1
    shares(0)
    while done < msgs:
        step(done)
        done += 1
    for i in (msgs - 2, msgs - 1):
        rs_r(i).wait_recv()
        rs_l(i).wait_recv()
    fin[pl.ds(0, half), :] = (
        both(0, 0) + rrecv[msgs - 1].astype(F32) + lrecv[msgs - 2].astype(F32)
    )
    fin[pl.ds(half, half), :] = (
        both(0, 1) + rrecv[msgs - 2].astype(F32) + lrecv[msgs - 1].astype(F32)
    )
    st_fin = pltpu.make_async_copy(fin, input_grad, ld_sem.at[5])
    st_fin.start()
    for dz in range(1, Z):
        remote(
            bk.at[zat(dz)], sliced(rt, z), pc_s.at[dz - 1], pc_r.at[dz - 1], zpeer(dz)
        ).wait_send()
    for s in range(Y):
        rsib(s).wait_send()
    for i in range(msgs):
        rs_r(i).wait_send()
        rs_l(i).wait_send()
    st_attn.wait()
    st_fin.wait()


def local(X, Z, Y, tokens, w_qkv, forget, out_grad, doc_lengths):
    R, F = tokens.shape
    D, C = w_qkv.shape[1:]
    heads = C // DH
    docs = doc_lengths.shape[0]
    TP = 2 * Y
    hops = Y // 2
    msgs = 2 * hops - 1
    half = R // 2
    SR = -(-2 * heads * DH // Z)
    SR = -(-SR // 16) * 16
    dma = pltpu.SemaphoreType.DMA
    V = pltpu.VMEM
    scratch = [
        V((3, D, C), BF16), V((TP, R, F), BF16), V((R, heads), F32), V((R, C), BF16),
        V((3, R, C), F32), V((3, R, C), BF16), V((R, C), F32), V((R, C), F32),
        V((heads, R, R), F32), V((heads, R, DH), F32), V((heads, R, DH), F32), V((4, R, C), F32),
        V((8, DH), F32), V((Z, 8, DH), F32), V((8, DH), F32), V((X, 8, DH), F32),
        V((Z, SR, DH), F32), V((Z, SR, DH), F32), V((Z, SR, DH), F32),
        V((Z * SR, DH), BF16), V((Z, SR, DH), BF16), V((SR, DH), BF16), V((X, SR, DH), BF16),
        V((Z, SR, DH), BF16), V((Z * SR, DH), BF16),
        V((Y, R, C), BF16), V((Y, R, C), BF16), V((Y, R, C), F32),
        V((msgs, half, C), BF16), V((msgs, half, C), BF16),
        V((msgs, half, C), BF16), V((msgs, half, C), BF16),
        dma((6,)),
        dma((msgs,)), dma((msgs,)), dma((msgs,)), dma((msgs,)),
        dma((2 * msgs + 1,)), dma((2 * msgs + 1,)),
        dma((Z - 1,)), dma((Z - 1,)), dma((X - 1,)), dma((X - 1,)),
        dma((Z - 1,)), dma((Z - 1,)), dma((X - 1,)), dma((X - 1,)),
        dma((Z - 1,)), dma((Z - 1,)),
        dma((Y,)), dma((Y,)), dma((msgs,)), dma((msgs,)), dma((msgs,)), dma((msgs,)),
    ]
    anywhere = pl.BlockSpec(memory_space=pl.ANY)
    return pl.pallas_call(
        functools.partial(kernel, X, Z, Y, R, C, SR, docs),
        out_shape=(
            jax.ShapeDtypeStruct((R, C), F32),
            jax.ShapeDtypeStruct((R, F), F32),
        ),
        in_specs=[anywhere] * 4 + [pl.BlockSpec(memory_space=pltpu.SMEM)],
        out_specs=(anywhere, anywhere),
        scratch_shapes=scratch,
        compiler_params=pltpu.CompilerParams(
            collective_id=0, has_side_effects=True, vmem_limit_bytes=48 * 1024 * 1024
        ),
        name="decayed_attention_step",
    )(tokens, w_qkv, forget, out_grad, doc_lengths)


X_CHIPS = 4


def solution(mesh, x_chips=X_CHIPS):
    seq, tp = mesh.shape["seq"], mesh.shape["tp"]
    placed = (P("seq", "tp"), P(None, None, "tp"), P("seq", "tp"), P("seq", "tp"), P())
    return jax.shard_map(
        functools.partial(local, x_chips, seq // x_chips, tp // 2),
        mesh=mesh,
        in_specs=placed,
        out_specs=(P("seq", "tp"), P("seq", "tp")),
        check_vma=False,
    )
```

```python
import functools

import jax
import jax.numpy as jnp
from jax import lax
from jax.experimental import pallas as pl
from jax.experimental.pallas import tpu as pltpu
from jax.sharding import PartitionSpec as P

DH = 128
CHUNKS = 4
F32 = jnp.float32
BF16 = jnp.bfloat16
MESH = pl.DeviceIdType.MESH


def dot_nn(a, b):
    return lax.dot_general(a, b, (((1,), (0,)), ((), ())), preferred_element_type=F32)


def dot_nt(a, b):
    return lax.dot_general(a, b, (((1,), (1,)), ((), ())), preferred_element_type=F32)


def dot_tn(a, b):
    return lax.dot_general(a, b, (((0,), (0,)), ((), ())), preferred_element_type=F32)


def kernel(
    X, Z, Y, R, C, SR, docs,
    tokens, w, forget, out_grad, doc_hbm,
    attn_out, input_grad,
    doc_lengths, wv, tok, fg, og, acc, qkv, gr, attn, fin,
    weight, lead, tail, part,
    lzs, lz, lxs, lx, coef, cum, pre,
    st, rc, ts, tx, bk, rt,
    sbs, sbr, own, rsend, rrecv, lsend, lrecv,
    ld_sem,
    agr_s, agr_r, agl_s, agl_r, sib_s, sib_r,
    e1_s, e1_r, e2_s, e2_r, pa_s, pa_r, pb_s, pb_r, pc_s, pc_r,
    rsib_s, rsib_r, rsr_s, rsr_r, rsl_s, rsl_r,
):
    heads = C // DH
    CH = CHUNKS
    piece = R // CH
    hops = Y // 2
    msgs = (hops - 1) * CH + CH // 2
    seq = lax.axis_index("seq")
    tp = lax.axis_index("tp")
    x = lax.div(seq, Z)
    z = lax.rem(seq, Z)
    y = lax.div(tp, 2)
    c = lax.rem(tp, 2)

    def chip(o):
        return lax.rem(y + (o + Y), Y)

    right = (seq, chip(1) * 2 + c)
    left = (seq, chip(-1) * 2 + c)
    sibling = (seq, y * 2 + (1 - c))

    def zat(dz):
        return lax.rem(z + dz, Z)

    def xat(dx):
        return lax.rem(x + dx, X)

    def zpeer(dz):
        return (x * Z + zat(dz), tp)

    def xpeer(dx):
        return (xat(dx) * Z + z, tp)

    def remote(src, dst, ssem, rsem, dev):
        return pltpu.make_async_remote_copy(
            src_ref=src, dst_ref=dst, send_sem=ssem, recv_sem=rsem,
            device_id=dev, device_id_type=MESH,
        )

    own_tok = tok.at[tp]
    ld_tok = pltpu.make_async_copy(tokens, own_tok, ld_sem.at[0])
    ld_fg = pltpu.make_async_copy(forget, fg, ld_sem.at[1])
    ld_w = pltpu.make_async_copy(w, wv, ld_sem.at[2])
    ld_og = pltpu.make_async_copy(out_grad, og, ld_sem.at[3])
    ld_tok.start()
    ld_fg.start()
    ld_w.start()
    ld_og.start()
    ld_doc = pltpu.make_async_copy(doc_hbm, doc_lengths, ld_sem.at[6])
    ld_doc.start()

    barrier = pltpu.get_barrier_semaphore()
    peers = [right, left, sibling]
    peers += [zpeer(dz) for dz in range(1, Z)]
    peers += [xpeer(dx) for dx in range(1, X)]
    for dev in peers:
        pl.semaphore_signal(barrier, inc=1, device_id=dev, device_id_type=MESH)
    pl.semaphore_wait(barrier, len(peers))

    def piece_of(ref, i):
        return ref.at[pl.ds(i * piece, piece)]

    def r_place(i, shift):
        return piece_of(tok.at[chip(-(i // CH) - shift) * 2 + c], i % CH)

    def l_place(i, shift):
        return piece_of(tok.at[chip(i // CH + shift) * 2 + c], CH - 1 - i % CH)

    ag_r = [remote(r_place(i, 0), r_place(i, 0), agr_s.at[i], agr_r.at[i], right) for i in range(msgs)]
    ag_l = [remote(l_place(i, 0), l_place(i, 0), agl_s.at[i], agl_r.at[i], left) for i in range(msgs)]
    in_r = [remote(r_place(i, 1), r_place(i, 1), agr_s.at[i], agr_r.at[i], right) for i in range(msgs)]
    in_l = [remote(l_place(i, 1), l_place(i, 1), agl_s.at[i], agl_r.at[i], left) for i in range(msgs)]

    def sib_place(k, core):
        if k == 0:
            return tok.at[y * 2 + core]
        if k <= msgs:
            i = k - 1
            return piece_of(tok.at[chip(-(i // CH) - 1) * 2 + core], i % CH)
        i = k - 1 - msgs
        return piece_of(tok.at[chip(i // CH + 1) * 2 + core], CH - 1 - i % CH)

    sib_out = [
        remote(sib_place(k, c), sib_place(k, c), sib_s.at[k], sib_r.at[k], sibling)
        for k in range(2 * msgs + 1)
    ]
    sib_in = [
        remote(sib_place(k, 1 - c), sib_place(k, 1 - c), sib_s.at[k], sib_r.at[k], sibling)
        for k in range(2 * msgs + 1)
    ]

    ld_tok.wait()
    for i in range(CH):
        ag_r[i].start()
        ag_l[i].start()
    sib_out[0].start()

    near = sorted(range(1, Z), key=lambda dz: -min(dz, Z - dz))
    ld_fg.wait()
    rows = lax.broadcasted_iota(jnp.int32, (R, R), 0)
    cols = lax.broadcasted_iota(jnp.int32, (R, R), 1)
    sums = []
    for h in range(heads):
        frow = jnp.broadcast_to(fg[h : h + 1, :], (R, R))
        lcol = jnp.sum(jnp.where(cols <= rows, frow, 0.0), axis=1, keepdims=True)
        lrow = jnp.sum(jnp.where(rows == cols, lcol, 0.0), axis=0, keepdims=True)
        sums.append((lcol, lrow, lrow[:, R - 1 : R]))
    row8 = lax.broadcasted_iota(jnp.int32, (8, DH), 0)
    lzs[...] = jnp.where(row8 == 0, sums[0][2], sums[1][2])
    e1 = [remote(lzs, lz.at[z], e1_s.at[dz - 1], e1_r.at[dz - 1], zpeer(dz)) for dz in near]
    for cp in e1:
        cp.start()
    lz[z] = lzs[...]

    ld_doc.wait()
    ends = []
    total = jnp.int32(0)
    for j in range(docs):
        total = total + doc_lengths[j]
        ends.append(total)
    offset = seq * R

    def doc_of(position):
        count = jnp.int32(0)
        for e in ends:
            count = count + jnp.where(position >= e, 1, 0).astype(jnp.int32)
        return count

    def weights():
        prior = jnp.where(offset > 0, doc_of(offset - 1), -1)
        last = doc_of(offset + R - 1)
        doc_row = doc_of(offset + lax.broadcasted_iota(jnp.int32, (1, R), 1))
        doc_col = doc_of(offset + lax.broadcasted_iota(jnp.int32, (R, 1), 0))
        mask = (doc_col == doc_row) & (rows >= cols)
        lane = (R, DH)
        for h in range(heads):
            lcol, lrow, ltot = sums[h]
            gap = jnp.where(mask, lcol - lrow, 0.0)
            weight[h] = jnp.where(mask, jnp.exp(gap), 0.0)
            lead[h] = jnp.broadcast_to(jnp.where(doc_col == prior, jnp.exp(lcol), 0.0), lane)
            tail[h] = jnp.broadcast_to(
                jnp.where(doc_col == last, jnp.exp(ltot - lcol), 0.0), lane
            )

    srow = lax.broadcasted_iota(jnp.int32, (SR, DH), 0) + z * SR
    is_back = srow >= heads * DH
    second = (lax.rem(srow, 2 * DH)) >= DH

    def decays():
        for dz in range(1, Z):
            src = lax.rem(z + (Z - dz), Z)
            remote(lzs, lz.at[src], e1_s.at[dz - 1], e1_r.at[dz - 1], zpeer(dz)).wait_recv()
        place = x * Z + lax.broadcasted_iota(jnp.int32, (16, DH), 0)
        through = place > 0
        for e in ends:
            through = through & jnp.logical_not((e >= place * R) & (e < place * R + R))
        thru = jnp.where(through, 1.0, 0.0)
        a = []
        for p in range(Z):
            v = lz[p]
            a.append([jnp.where(thru[p : p + 1] > 0, jnp.exp(v[h : h + 1]), 0.0) for h in range(heads)])
        up = [jnp.ones((1, DH), F32)] * heads
        for p in range(Z):
            coef[p] = jnp.where(second, a[p][1], a[p][0])
            cum[p] = jnp.where(second, up[1], up[0])
            up = [up[h] * a[p][h] for h in range(heads)]
        down = [jnp.ones((1, DH), F32)] * heads
        for p in reversed(range(Z)):
            cum[p] = jnp.where(is_back, jnp.where(second, down[1], down[0]), cum[p])
            down = [down[h] * a[p][h] for h in range(heads)]
        lxs[...] = jnp.where(row8 == 0, up[0], up[1])
        lx[x] = lxs[...]
        for dx in range(1, X):
            remote(lxs, lx.at[x], e2_s.at[dx - 1], e2_r.at[dx - 1], xpeer(dx)).start()

    def block_term(j, m):
        return dot_nn(tok[j], wv[m, pl.ds(pl.multiple_of(j * C, C), C), :])

    def project_hop(k):
        for m in range(3):
            out = None
            for o in [0] if k == 0 else [-k, k]:
                for core in range(2):
                    term = block_term(chip(o) * 2 + core, m)
                    out = term if out is None else out + term
            acc[m] = out if k == 0 else acc[m] + out

    def sib_wait(k):
        if k == 0:
            sib_in[0].wait_recv()
            return
        for i in range((k - 1) * CH, min(k * CH, msgs)):
            sib_in[1 + i].wait_recv()
            sib_in[1 + msgs + i].wait_recv()

    for k in range(1, hops + 1):
        for i in range((k - 1) * CH, min(k * CH, msgs)):
            in_r[i].wait_recv()
            if i + CH < msgs:
                ag_r[i + CH].start()
            sib_out[1 + i].start()
            in_l[i].wait_recv()
            if i + CH < msgs:
                ag_l[i + CH].start()
            sib_out[1 + msgs + i].start()
        if k == 1:
            weights()
            ld_w.wait()
            ld_og.wait()
        if k == hops - 1:
            decays()
        sib_wait(k - 1)
        project_hop(k - 1)

    far = chip(hops) * 2
    for m in (1, 2, 0):
        acc[m] += block_term(far + c, m)
    sib_wait(hops)
    for m in (1, 2, 0):
        qkv[m] = (acc[m] + block_term(far + 1 - c, m)).astype(BF16)

    def head(m, h):
        return qkv[m, :, pl.ds(h * DH, DH)]

    def grad_head(h):
        return og[:, pl.ds(h * DH, DH)]

    for h in range(heads):
        kt = (head(1, h).astype(F32) * tail[h]).astype(BF16)
        st[pl.ds(h * DH, DH), :] = dot_tn(kt, head(2, h)).astype(BF16)
        ql = (head(0, h).astype(F32) * lead[h]).astype(BF16)
        st[pl.ds((heads + h) * DH, DH), :] = (
            dot_tn(ql, grad_head(h)) * (1.0 / DH)
        ).astype(BF16)
    if Z * SR > 2 * heads * DH:
        spare = Z * SR - 2 * heads * DH
        st[pl.ds(2 * heads * DH, spare), :] = jnp.zeros((spare, DH), BF16)

    def sliced(ref, p):
        return ref.at[pl.ds(pl.multiple_of(p * SR, SR), SR)]

    for dz in near:
        remote(
            sliced(st, zat(dz)), rc.at[z], pa_s.at[dz - 1], pa_r.at[dz - 1], zpeer(dz)
        ).start()
    rc[z] = st[pl.ds(pl.multiple_of(z * SR, SR), SR), :]

    def two_terms(value):
        high = value.astype(BF16)
        return high, (value - high.astype(F32)).astype(BF16)

    def inside(h):
        q, k, v, g = head(0, h), head(1, h), head(2, h), grad_head(h)
        cols_h = pl.ds(h * DH, DH)
        a, a2 = two_terms(dot_nt(q, k) * weight[h])
        b, b2 = two_terms(dot_nt(g, v) * weight[h])
        part[0, :, cols_h] = dot_nn(a, v) + dot_nn(a2, v)
        part[1, :, cols_h] = dot_nn(b, k) + dot_nn(b2, k)
        part[2, :, cols_h] = dot_tn(b, q) + dot_tn(b2, q)
        part[3, :, cols_h] = dot_tn(a, g) + dot_tn(a2, g)

    inside(0)

    for dz in range(1, Z):
        src = lax.rem(z + (Z - dz), Z)
        remote(
            sliced(st, src), rc.at[src], pa_s.at[dz - 1], pa_r.at[dz - 1], zpeer(dz)
        ).wait_recv()
    run = jnp.zeros((SR, DH), F32)
    for p in range(Z):
        pre[p] = run
        run = coef[p] * run + rc[p].astype(F32)
    back = jnp.zeros((SR, DH), F32)
    for p in reversed(range(Z)):
        pre[p] = jnp.where(is_back, back, pre[p])
        back = coef[p] * back + rc[p].astype(F32)
    ts[...] = jnp.where(is_back, back, run).astype(BF16)
    tx[x] = ts[...]
    for dx in range(1, X):
        remote(ts, tx.at[x], pb_s.at[dx - 1], pb_r.at[dx - 1], xpeer(dx)).start()

    inside(1)

    for dx in range(1, X):
        src = lax.rem(x + (X - dx), X)
        remote(lxs, lx.at[src], e2_s.at[dx - 1], e2_r.at[dx - 1], xpeer(dx)).wait_recv()
        remote(ts, tx.at[src], pb_s.at[dx - 1], pb_r.at[dx - 1], xpeer(dx)).wait_recv()
    run = jnp.zeros((SR, DH), F32)
    back = jnp.zeros((SR, DH), F32)
    for p in range(X):
        v = lx[p]
        line = jnp.where(second, v[1:2], v[0:1])
        run = jnp.where(x > p, line * run + tx[p].astype(F32), run)
    for p in reversed(range(X)):
        v = lx[p]
        line = jnp.where(second, v[1:2], v[0:1])
        back = jnp.where(x < p, line * back + tx[p].astype(F32), back)
    carry = jnp.where(is_back, back, run)
    for p in range(Z):
        bk[p] = (pre[p] + cum[p] * carry).astype(BF16)
    for dz in near:
        remote(
            bk.at[zat(dz)], sliced(rt, z), pc_s.at[dz - 1], pc_r.at[dz - 1], zpeer(dz)
        ).start()
    rt[pl.ds(pl.multiple_of(z * SR, SR), SR), :] = bk[z]

    for cp in ag_r + ag_l + sib_out + e1:
        cp.wait_send()
    for dx in range(1, X):
        remote(lxs, lx.at[x], e2_s.at[dx - 1], e2_r.at[dx - 1], xpeer(dx)).wait_send()
        remote(ts, tx.at[x], pb_s.at[dx - 1], pb_r.at[dx - 1], xpeer(dx)).wait_send()
    for dz in near:
        remote(
            sliced(st, zat(dz)), rc.at[z], pa_s.at[dz - 1], pa_r.at[dz - 1], zpeer(dz)
        ).wait_send()

    for dz in range(1, Z):
        src = lax.rem(z + (Z - dz), Z)
        remote(
            bk.at[src], sliced(rt, src), pc_s.at[dz - 1], pc_r.at[dz - 1], zpeer(dz)
        ).wait_recv()

    scale = 1.0 / DH
    for h in range(heads):
        q, k, v, g = head(0, h), head(1, h), head(2, h), grad_head(h)
        cols_h = pl.ds(h * DH, DH)
        state = rt[pl.ds(h * DH, DH), :]
        after = rt[pl.ds((heads + h) * DH, DH), :]
        gr[0, :, cols_h] = (
            (part[1, :, cols_h] + lead[h] * dot_nt(g, state)) * scale
        ).astype(BF16)
        gr[1, :, cols_h] = (
            part[2, :, cols_h] * scale + tail[h] * dot_nt(v, after)
        ).astype(BF16)
        gr[2, :, cols_h] = (
            part[3, :, cols_h] * scale + tail[h] * dot_nn(k, after)
        ).astype(BF16)
        attn[:, cols_h] = (part[0, :, cols_h] + lead[h] * dot_nn(q, state)) * scale
    st_attn = pltpu.make_async_copy(attn, attn_out, ld_sem.at[4])
    st_attn.start()

    order = [hops]
    for k in reversed(range(1, hops)):
        order += [k, -k]
    order.append(0)
    slot = {o: i for i, o in enumerate(order)}
    slot[-hops] = slot[hops]

    def share(j):
        out = None
        for m in range(3):
            term = dot_nt(gr[m], wv[m, pl.ds(pl.multiple_of(j * C, C), C), :])
            out = term if out is None else out + term
        return out

    def rsib(s):
        return remote(sbs.at[s], sbr.at[s], rsib_s.at[s], rsib_r.at[s], sibling)

    def for_sibling(o):
        sbs[slot[o]] = share(chip(o) * 2 + (1 - c))
        rsib(slot[o]).start()

    def for_ring(o):
        own[slot[o]] = share(chip(o) * 2 + c)

    joined = set()

    def both(o, i):
        s = slot[o]
        if s not in joined:
            rsib(s).wait_recv()
            joined.add(s)
        part_rows = pl.ds(i * piece, piece)
        return own[s, part_rows, :] + sbr[s, part_rows, :]

    def rs_r(i):
        return remote(rsend.at[i], rrecv.at[i], rsr_s.at[i], rsr_r.at[i], right)

    def rs_l(i):
        return remote(lsend.at[i], lrecv.at[i], rsl_s.at[i], rsl_r.at[i], left)

    ring = [(hops, i) for i in range(CH // 2)]
    turned = [*range(CH // 2, CH), *range(CH // 2)]
    for k in reversed(range(1, hops)):
        ring += [(k, i) for i in turned]

    def step(n):
        o, i = ring[n]
        value = both(o, i)
        if n >= CH:
            rs_r(n - CH).wait_recv()
            value = value + rrecv[n - CH].astype(F32)
        rsend[n] = value.astype(BF16)
        rs_r(n).start()
        value = both(-o, CH - 1 - i)
        if n >= CH:
            rs_l(n - CH).wait_recv()
            value = value + lrecv[n - CH].astype(F32)
        lsend[n] = value.astype(BF16)
        rs_l(n).start()

    for_sibling(hops)
    for_sibling(hops - 1)
    for_ring(hops)
    for n in range(CH // 2):
        step(n)
    for_sibling(1 - hops)
    for_ring(hops - 1)
    for_ring(1 - hops)
    for n in range(CH // 2, CH):
        step(n)
    done = CH
    for k in reversed(range(hops - 1)):
        for o in [k, -k] if k else [0]:
            for_sibling(o)
        for o in [k, -k] if k else [0]:
            for_ring(o)
        for n in range(done, min(done + CH, msgs)):
            step(n)
        done = min(done + CH, msgs)
    base = msgs - CH
    for i in turned:
        n_r = base + turned.index(i)
        n_l = base + turned.index(CH - 1 - i)
        value = both(0, i)
        rs_r(n_r).wait_recv()
        rs_l(n_l).wait_recv()
        fin[pl.ds(i * piece, piece), :] = (
            value + rrecv[n_r].astype(F32) + lrecv[n_l].astype(F32)
        )
    st_fin = pltpu.make_async_copy(fin, input_grad, ld_sem.at[5])
    st_fin.start()
    for dz in range(1, Z):
        remote(
            bk.at[zat(dz)], sliced(rt, z), pc_s.at[dz - 1], pc_r.at[dz - 1], zpeer(dz)
        ).wait_send()
    for s in range(Y):
        rsib(s).wait_send()
    for i in range(msgs):
        rs_r(i).wait_send()
        rs_l(i).wait_send()
    st_attn.wait()
    st_fin.wait()


def local(X, Z, Y, tokens, w_qkv, forget, out_grad, doc_lengths):
    R, F = tokens.shape
    D, C = w_qkv.shape[1:]
    heads = C // DH
    docs = doc_lengths.shape[0]
    TP = 2 * Y
    hops = Y // 2
    msgs = (hops - 1) * CHUNKS + CHUNKS // 2
    piece = R // CHUNKS
    SR = -(-2 * heads * DH // Z)
    SR = -(-SR // 16) * 16
    dma = pltpu.SemaphoreType.DMA
    V = pltpu.VMEM
    scratch = [
        pltpu.SMEM((docs,), jnp.int32),
        V((3, D, C), BF16), V((TP, R, F), BF16), V((heads, R), F32), V((R, C), BF16),
        V((3, R, C), F32), V((3, R, C), BF16), V((3, R, C), BF16), V((R, C), F32), V((R, C), F32),
        V((heads, R, R), F32), V((heads, R, DH), F32), V((heads, R, DH), F32), V((4, R, C), F32),
        V((8, DH), F32), V((Z, 8, DH), F32), V((8, DH), F32), V((X, 8, DH), F32),
        V((Z, SR, DH), F32), V((Z, SR, DH), F32), V((Z, SR, DH), F32),
        V((Z * SR, DH), BF16), V((Z, SR, DH), BF16), V((SR, DH), BF16), V((X, SR, DH), BF16),
        V((Z, SR, DH), BF16), V((Z * SR, DH), BF16),
        V((Y, R, C), F32), V((Y, R, C), F32), V((Y, R, C), F32),
        V((msgs, piece, C), BF16), V((msgs, piece, C), BF16),
        V((msgs, piece, C), BF16), V((msgs, piece, C), BF16),
        dma((7,)),
        dma((msgs,)), dma((msgs,)), dma((msgs,)), dma((msgs,)),
        dma((2 * msgs + 1,)), dma((2 * msgs + 1,)),
        dma((Z - 1,)), dma((Z - 1,)), dma((X - 1,)), dma((X - 1,)),
        dma((Z - 1,)), dma((Z - 1,)), dma((X - 1,)), dma((X - 1,)),
        dma((Z - 1,)), dma((Z - 1,)),
        dma((Y,)), dma((Y,)), dma((msgs,)), dma((msgs,)), dma((msgs,)), dma((msgs,)),
    ]
    anywhere = pl.BlockSpec(memory_space=pltpu.HBM)
    return pl.pallas_call(
        functools.partial(kernel, X, Z, Y, R, C, SR, docs),
        out_shape=(
            jax.ShapeDtypeStruct((R, C), F32),
            jax.ShapeDtypeStruct((R, F), F32),
        ),
        in_specs=[anywhere] * 5,
        out_specs=(anywhere, anywhere),
        scratch_shapes=scratch,
        compiler_params=pltpu.CompilerParams(
            collective_id=0, has_side_effects=True, vmem_limit_bytes=64 * 1024 * 1024
        ),
        name="decayed_attention_step",
    )(tokens, w_qkv, forget.T, out_grad, doc_lengths)


X_CHIPS = 4


def solution(mesh, x_chips=X_CHIPS):
    seq, tp = mesh.shape["seq"], mesh.shape["tp"]
    placed = (P("seq", "tp"), P(None, None, "tp"), P("seq", "tp"), P("seq", "tp"), P())
    return jax.shard_map(
        functools.partial(local, x_chips, seq // x_chips, tp // 2),
        mesh=mesh,
        in_specs=placed,
        out_specs=(P("seq", "tp"), P("seq", "tp")),
        check_vma=False,
    )
```

```python
import functools

import jax
import jax.numpy as jnp
from jax import lax
from jax.experimental import pallas as pl
from jax.experimental.pallas import tpu as pltpu
from jax.sharding import PartitionSpec as P

DH = 128
CHUNKS = 4
F32 = jnp.float32
BF16 = jnp.bfloat16
MESH = pl.DeviceIdType.MESH


def dot_nn(a, b):
    return lax.dot_general(a, b, (((1,), (0,)), ((), ())), preferred_element_type=F32)


def dot_nt(a, b):
    return lax.dot_general(a, b, (((1,), (1,)), ((), ())), preferred_element_type=F32)


def dot_tn(a, b):
    return lax.dot_general(a, b, (((0,), (0,)), ((), ())), preferred_element_type=F32)


def kernel(
    X, Z, Y, R, C, SR, docs,
    tokens, w, forget, out_grad, doc_hbm,
    attn_out, input_grad,
    doc_lengths, wv, tok, fg, og, acc, qkv, gr, attn, fin,
    weight, lead, tail, part,
    lzs, lz, lxs, lx, coef, cum, share_of, pre,
    st, rc, ts, tx, bk, rt,
    sbs, sbr, own, rsend, rrecv, lsend, lrecv,
    ld_sem,
    agr_s, agr_r, agl_s, agl_r, sib_s, sib_r,
    e1_s, e1_r, e2_s, e2_r, pa_s, pa_r, pb_s, pb_r, pc_s, pc_r,
    rsib_s, rsib_r, rsr_s, rsr_r, rsl_s, rsl_r,
    xr, xl, xr_s, xr_r, xl_s, xl_r,
):
    heads = C // DH
    CH = CHUNKS
    piece = R // CH
    hops = Y // 2
    msgs = (hops - 1) * CH + CH // 2
    seq = lax.axis_index("seq")
    tp = lax.axis_index("tp")
    x = lax.div(seq, Z)
    z = lax.rem(seq, Z)
    y = lax.div(tp, 2)
    c = lax.rem(tp, 2)

    def chip(o):
        return lax.rem(y + (o + Y), Y)

    right = (seq, chip(1) * 2 + c)
    left = (seq, chip(-1) * 2 + c)
    sibling = (seq, y * 2 + (1 - c))
    right_x = (seq, chip(1) * 2 + (1 - c))
    left_x = (seq, chip(-1) * 2 + (1 - c))

    def zat(dz):
        return lax.rem(z + dz, Z)

    def xat(dx):
        return lax.rem(x + dx, X)

    def zpeer(dz):
        return (x * Z + zat(dz), tp)

    def xpeer(dx):
        return (xat(dx) * Z + z, tp)

    def remote(src, dst, ssem, rsem, dev):
        return pltpu.make_async_remote_copy(
            src_ref=src, dst_ref=dst, send_sem=ssem, recv_sem=rsem,
            device_id=dev, device_id_type=MESH,
        )

    own_tok = tok.at[tp]
    ld_tok = pltpu.make_async_copy(tokens, own_tok, ld_sem.at[0])
    ld_fg = pltpu.make_async_copy(forget, fg, ld_sem.at[1])
    ld_w = pltpu.make_async_copy(w, wv, ld_sem.at[2])
    ld_og = pltpu.make_async_copy(out_grad, og, ld_sem.at[3])
    ld_tok.start()
    ld_fg.start()
    ld_w.start()
    ld_og.start()
    ld_doc = pltpu.make_async_copy(doc_hbm, doc_lengths, ld_sem.at[6])
    ld_doc.start()

    barrier = pltpu.get_barrier_semaphore()
    peers = [right, left, sibling, right_x, left_x]
    peers += [zpeer(dz) for dz in range(1, Z)]
    peers += [xpeer(dx) for dx in range(1, X)]
    for dev in peers:
        pl.semaphore_signal(barrier, inc=1, device_id=dev, device_id_type=MESH)
    pl.semaphore_wait(barrier, len(peers))

    def piece_of(ref, i):
        return ref.at[pl.ds(i * piece, piece)]

    def r_place(i, shift):
        return piece_of(tok.at[chip(-(i // CH) - shift) * 2 + c], i % CH)

    def l_place(i, shift):
        return piece_of(tok.at[chip(i // CH + shift) * 2 + c], CH - 1 - i % CH)

    def r_source(i):
        return piece_of(tokens, i) if i < CH else r_place(i, 0)

    def l_source(i):
        return piece_of(tokens, CH - 1 - i) if i < CH else l_place(i, 0)

    ag_r = [remote(r_source(i), r_place(i, 0), agr_s.at[i], agr_r.at[i], right) for i in range(msgs)]
    ag_l = [remote(l_source(i), l_place(i, 0), agl_s.at[i], agl_r.at[i], left) for i in range(msgs)]
    in_r = [remote(r_place(i, 1), r_place(i, 1), agr_s.at[i], agr_r.at[i], right) for i in range(msgs)]
    in_l = [remote(l_place(i, 1), l_place(i, 1), agl_s.at[i], agl_r.at[i], left) for i in range(msgs)]

    def sib_place(k, core):
        if k == 0:
            return tok.at[y * 2 + core]
        if k <= msgs:
            i = k - 1
            return piece_of(tok.at[chip(-(i // CH) - 1) * 2 + core], i % CH)
        i = k - 1 - msgs
        return piece_of(tok.at[chip(i // CH + 1) * 2 + core], CH - 1 - i % CH)

    sib_out = [
        remote(sib_place(k, c) if k else tokens, sib_place(k, c), sib_s.at[k], sib_r.at[k], sibling)
        for k in range(2 * msgs + 1)
    ]
    last_hop = (hops - 1) * CH
    for i in range(last_hop, msgs):
        k = 1 + i
        sib_out[k] = remote(r_place(i, 0), r_place(i, 0), sib_s.at[k], sib_r.at[k], right_x)
        k = 1 + msgs + i
        sib_out[k] = remote(l_place(i, 0), l_place(i, 0), sib_s.at[k], sib_r.at[k], left_x)
    sib_in = [
        remote(sib_place(k, 1 - c), sib_place(k, 1 - c), sib_s.at[k], sib_r.at[k], sibling)
        for k in range(2 * msgs + 1)
    ]

    for i in range(CH):
        ag_r[i].start()
        ag_l[i].start()
    sib_out[0].start()

    near = sorted(range(1, Z), key=lambda dz: -min(dz, Z - dz))
    across = sorted(range(1, X), key=lambda dx: -min(dx, X - dx))
    ld_fg.wait()
    rows = lax.broadcasted_iota(jnp.int32, (R, R), 0)
    cols = lax.broadcasted_iota(jnp.int32, (R, R), 1)
    sums = []
    for h in range(heads):
        frow = jnp.broadcast_to(fg[h : h + 1, :], (R, R))
        lcol = jnp.sum(jnp.where(cols <= rows, frow, 0.0), axis=1, keepdims=True)
        lrow = jnp.sum(jnp.where(rows == cols, lcol, 0.0), axis=0, keepdims=True)
        sums.append((lcol, lrow, lrow[:, R - 1 : R]))
    row8 = lax.broadcasted_iota(jnp.int32, (8, DH), 0)
    lzs[...] = jnp.where(row8 == 0, sums[0][2], sums[1][2])
    e1 = [remote(lzs, lz.at[z], e1_s.at[dz - 1], e1_r.at[dz - 1], zpeer(dz)) for dz in near]
    for cp in e1:
        cp.start()
    lz[z] = lzs[...]

    ld_doc.wait()
    ends = []
    total = jnp.int32(0)
    for j in range(docs):
        total = total + doc_lengths[j]
        ends.append(total)
    offset = seq * R

    def doc_of(position):
        count = jnp.int32(0)
        for e in ends:
            count = count + jnp.where(position >= e, 1, 0).astype(jnp.int32)
        return count

    def weights():
        prior = jnp.where(offset > 0, doc_of(offset - 1), -1)
        last = doc_of(offset + R - 1)
        doc_row = doc_of(offset + lax.broadcasted_iota(jnp.int32, (1, R), 1))
        doc_col = doc_of(offset + lax.broadcasted_iota(jnp.int32, (R, 1), 0))
        mask = (doc_col == doc_row) & (rows >= cols)
        lane = (R, DH)
        for h in range(heads):
            lcol, lrow, ltot = sums[h]
            gap = jnp.where(mask, lcol - lrow, 0.0)
            weight[h] = jnp.where(mask, jnp.exp(gap), 0.0)
            lead[h] = jnp.broadcast_to(jnp.where(doc_col == prior, jnp.exp(lcol), 0.0), lane)
            tail[h] = jnp.broadcast_to(
                jnp.where(doc_col == last, jnp.exp(ltot - lcol), 0.0), lane
            )

    srow = lax.broadcasted_iota(jnp.int32, (SR, DH), 0) + z * SR
    is_back = srow >= heads * DH
    second = (lax.rem(srow, 2 * DH)) >= DH

    def decays():
        for dz in range(1, Z):
            src = lax.rem(z + (Z - dz), Z)
            remote(lzs, lz.at[src], e1_s.at[dz - 1], e1_r.at[dz - 1], zpeer(dz)).wait_recv()
        place = x * Z + lax.broadcasted_iota(jnp.int32, (16, DH), 0)
        through = place > 0
        for e in ends:
            through = through & jnp.logical_not((e >= place * R) & (e < place * R + R))
        thru = jnp.where(through, 1.0, 0.0)
        a = []
        for p in range(Z):
            v = lz[p]
            a.append([jnp.where(thru[p : p + 1] > 0, jnp.exp(v[h : h + 1]), 0.0) for h in range(heads)])
        up = [jnp.ones((1, DH), F32)] * heads
        for p in range(Z):
            coef[p] = jnp.where(second, a[p][1], a[p][0])
            cum[p] = jnp.where(second, up[1], up[0])
            share_of[p] = cum[p]
            up = [up[h] * a[p][h] for h in range(heads)]
        down = [jnp.ones((1, DH), F32)] * heads
        for p in reversed(range(Z)):
            below = jnp.where(second, down[1], down[0])
            share_of[p] = jnp.where(is_back, share_of[p], below)
            cum[p] = jnp.where(is_back, below, cum[p])
            down = [down[h] * a[p][h] for h in range(heads)]
        lxs[...] = jnp.where(row8 == 0, up[0], up[1])
        lx[x] = lxs[...]
        for dx in across:
            remote(lxs, lx.at[x], e2_s.at[dx - 1], e2_r.at[dx - 1], xpeer(dx)).start()

    def block_term(j, m):
        return dot_nn(tok[j], wv[m, pl.ds(pl.multiple_of(j * C, C), C), :])

    def project_hop(k):
        for m in range(3):
            out = None
            for o in [0] if k == 0 else [-k, k]:
                for core in range(2):
                    term = block_term(chip(o) * 2 + core, m)
                    out = term if out is None else out + term
            acc[m] = out if k == 0 else acc[m] + out

    def sib_wait(k):
        if k == 0:
            sib_in[0].wait_recv()
            return
        for i in range((k - 1) * CH, min(k * CH, msgs)):
            sib_in[1 + i].wait_recv()
            sib_in[1 + msgs + i].wait_recv()

    for k in range(1, hops + 1):
        for i in range((k - 1) * CH, min(k * CH, msgs)):
            in_r[i].wait_recv()
            if i + CH < msgs:
                ag_r[i + CH].start()
            if last_hop <= i + CH < msgs:
                sib_out[1 + i + CH].start()
            if i < last_hop:
                sib_out[1 + i].start()
            in_l[i].wait_recv()
            if i + CH < msgs:
                ag_l[i + CH].start()
            if last_hop <= i + CH < msgs:
                sib_out[1 + msgs + i + CH].start()
            if i < last_hop:
                sib_out[1 + msgs + i].start()
        if k == 1:
            weights()
            ld_tok.wait()
            ld_w.wait()
            ld_og.wait()
        if k == hops - 1:
            decays()
        sib_wait(k - 1)
        project_hop(k - 1)

    far = chip(hops) * 2
    for m in (1, 2, 0):
        acc[m] += block_term(far + c, m)
    sib_wait(hops)
    for m in (1, 2, 0):
        qkv[m] = (acc[m] + block_term(far + 1 - c, m)).astype(BF16)

    def head(m, h):
        return qkv[m, :, pl.ds(h * DH, DH)]

    def grad_head(h):
        return og[:, pl.ds(h * DH, DH)]

    for h in range(heads):
        kt = (head(1, h).astype(F32) * tail[h]).astype(BF16)
        st[pl.ds(h * DH, DH), :] = dot_tn(kt, head(2, h)).astype(BF16)
        ql = (head(0, h).astype(F32) * lead[h]).astype(BF16)
        st[pl.ds((heads + h) * DH, DH), :] = (
            dot_tn(ql, grad_head(h)) * (1.0 / DH)
        ).astype(BF16)
    if Z * SR > 2 * heads * DH:
        spare = Z * SR - 2 * heads * DH
        st[pl.ds(2 * heads * DH, spare), :] = jnp.zeros((spare, DH), BF16)

    def sliced(ref, p):
        return ref.at[pl.ds(pl.multiple_of(p * SR, SR), SR)]

    for dz in near:
        remote(
            sliced(st, zat(dz)), rc.at[z], pa_s.at[dz - 1], pa_r.at[dz - 1], zpeer(dz)
        ).start()
    rc[z] = st[pl.ds(pl.multiple_of(z * SR, SR), SR), :]

    def two_terms(value):
        high = value.astype(BF16)
        return high, (value - high.astype(F32)).astype(BF16)

    def inside(h):
        q, k, v, g = head(0, h), head(1, h), head(2, h), grad_head(h)
        cols_h = pl.ds(h * DH, DH)
        a, a2 = two_terms(dot_nt(q, k) * weight[h])
        b, b2 = two_terms(dot_nt(g, v) * weight[h])
        part[0, :, cols_h] = dot_nn(a, v) + dot_nn(a2, v)
        part[1, :, cols_h] = dot_nn(b, k) + dot_nn(b2, k)
        part[2, :, cols_h] = dot_tn(b, q) + dot_tn(b2, q)
        part[3, :, cols_h] = dot_tn(a, g) + dot_tn(a2, g)

    for h in range(heads):
        inside(h)

    for dz in range(1, Z):
        src = lax.rem(z + (Z - dz), Z)
        remote(
            sliced(st, src), rc.at[src], pa_s.at[dz - 1], pa_r.at[dz - 1], zpeer(dz)
        ).wait_recv()
    line_total = share_of[0] * rc[0].astype(F32)
    for p in range(1, Z):
        line_total = line_total + share_of[p] * rc[p].astype(F32)
    ts[...] = line_total.astype(BF16)
    for dx in across:
        remote(ts, tx.at[x], pb_s.at[dx - 1], pb_r.at[dx - 1], xpeer(dx)).start()
    tx[x] = ts[...]

    run = jnp.zeros((SR, DH), F32)
    for p in range(Z):
        pre[p] = run
        run = coef[p] * run + rc[p].astype(F32)
    back = jnp.zeros((SR, DH), F32)
    for p in reversed(range(Z)):
        pre[p] = jnp.where(is_back, back, pre[p])
        back = coef[p] * back + rc[p].astype(F32)

    for dx in range(1, X):
        src = lax.rem(x + (X - dx), X)
        remote(lxs, lx.at[src], e2_s.at[dx - 1], e2_r.at[dx - 1], xpeer(dx)).wait_recv()
        remote(ts, tx.at[src], pb_s.at[dx - 1], pb_r.at[dx - 1], xpeer(dx)).wait_recv()
    run = jnp.zeros((SR, DH), F32)
    back = jnp.zeros((SR, DH), F32)
    for p in range(X):
        v = lx[p]
        line = jnp.where(second, v[1:2], v[0:1])
        run = jnp.where(x > p, line * run + tx[p].astype(F32), run)
    for p in reversed(range(X)):
        v = lx[p]
        line = jnp.where(second, v[1:2], v[0:1])
        back = jnp.where(x < p, line * back + tx[p].astype(F32), back)
    carry = jnp.where(is_back, back, run)

    def entering(p):
        bk[p] = (pre[p] + cum[p] * carry).astype(BF16)

    for dz in near:
        entering(zat(dz))
        remote(
            bk.at[zat(dz)], sliced(rt, z), pc_s.at[dz - 1], pc_r.at[dz - 1], zpeer(dz)
        ).start()
    entering(z)
    rt[pl.ds(pl.multiple_of(z * SR, SR), SR), :] = bk[z]

    for cp in ag_r + ag_l + sib_out + e1:
        cp.wait_send()
    for dx in range(1, X):
        remote(lxs, lx.at[x], e2_s.at[dx - 1], e2_r.at[dx - 1], xpeer(dx)).wait_send()
        remote(ts, tx.at[x], pb_s.at[dx - 1], pb_r.at[dx - 1], xpeer(dx)).wait_send()
    for dz in near:
        remote(
            sliced(st, zat(dz)), rc.at[z], pa_s.at[dz - 1], pa_r.at[dz - 1], zpeer(dz)
        ).wait_send()

    for dz in range(1, Z):
        src = lax.rem(z + (Z - dz), Z)
        remote(
            bk.at[src], sliced(rt, src), pc_s.at[dz - 1], pc_r.at[dz - 1], zpeer(dz)
        ).wait_recv()

    scale = 1.0 / DH
    for h in range(heads):
        k, v, g = head(1, h), head(2, h), grad_head(h)
        cols_h = pl.ds(h * DH, DH)
        state = rt[pl.ds(h * DH, DH), :]
        after = rt[pl.ds((heads + h) * DH, DH), :]
        gr[0, :, cols_h] = (
            (part[1, :, cols_h] + lead[h] * dot_nt(g, state)) * scale
        ).astype(BF16)
        gr[1, :, cols_h] = (
            part[2, :, cols_h] * scale + tail[h] * dot_nt(v, after)
        ).astype(BF16)
        gr[2, :, cols_h] = (
            part[3, :, cols_h] * scale + tail[h] * dot_nn(k, after)
        ).astype(BF16)

    order = [hops]
    for k in reversed(range(1, hops)):
        order += [k, -k]
    order.append(0)
    slot = {o: i for i, o in enumerate(order)}
    slot[-hops] = slot[hops]

    def share(j):
        out = None
        for m in range(3):
            term = dot_nt(gr[m], wv[m, pl.ds(pl.multiple_of(j * C, C), C), :])
            out = term if out is None else out + term
        return out

    def rsib(s):
        return remote(sbs.at[s], sbr.at[s], rsib_s.at[s], rsib_r.at[s], sibling)

    def x_r(n):
        return remote(piece_of(sbs.at[0], n), xr.at[n], xr_s.at[n], xr_r.at[n], right_x)

    def x_l(n):
        return remote(piece_of(sbs.at[0], CH - 1 - n), xl.at[n], xl_s.at[n], xl_r.at[n], left_x)

    def for_sibling(o):
        sbs[slot[o]] = share(chip(o) * 2 + (1 - c)).astype(BF16)
        rsib(slot[o]).start()

    def for_ring(o):
        own[slot[o]] = share(chip(o) * 2 + c)

    joined = set()

    def both(o, i):
        s = slot[o]
        if s == 0:
            return own[s, pl.ds(i * piece, piece), :]
        if s not in joined:
            rsib(s).wait_recv()
            joined.add(s)
        part_rows = pl.ds(i * piece, piece)
        return own[s, part_rows, :] + sbr[s, part_rows, :].astype(F32)

    def rs_r(i):
        return remote(rsend.at[i], rrecv.at[i], rsr_s.at[i], rsr_r.at[i], right)

    def rs_l(i):
        return remote(lsend.at[i], lrecv.at[i], rsl_s.at[i], rsl_r.at[i], left)

    ring = [(hops, i) for i in range(CH // 2)]
    turned = [*range(CH // 2, CH), *range(CH // 2)]
    for k in reversed(range(1, hops)):
        ring += [(k, i) for i in turned]

    def step(n):
        o, i = ring[n]
        value = both(o, i)
        if n >= CH:
            rs_r(n - CH).wait_recv()
            value = value + rrecv[n - CH].astype(F32)
            if n - CH < CH // 2:
                x_r(n - CH).wait_recv()
                value = value + xr[n - CH].astype(F32)
        rsend[n] = value.astype(BF16)
        rs_r(n).start()
        value = both(-o, CH - 1 - i)
        if n >= CH:
            rs_l(n - CH).wait_recv()
            value = value + lrecv[n - CH].astype(F32)
            if n - CH < CH // 2:
                x_l(n - CH).wait_recv()
                value = value + xl[n - CH].astype(F32)
        lsend[n] = value.astype(BF16)
        rs_l(n).start()

    sbs[0] = share(chip(hops) * 2 + (1 - c)).astype(BF16)
    for n in range(CH // 2):
        x_r(n).start()
        x_l(n).start()
    for_ring(hops)
    for n in range(CH // 2):
        step(n)
    for_sibling(hops - 1)
    for_sibling(1 - hops)
    for_ring(hops - 1)
    for_ring(1 - hops)
    for n in range(CH // 2, CH):
        step(n)
    for h in range(heads):
        cols_h = pl.ds(h * DH, DH)
        state = rt[pl.ds(h * DH, DH), :]
        attn[:, cols_h] = (part[0, :, cols_h] + lead[h] * dot_nn(head(0, h), state)) * scale
    st_attn = pltpu.make_async_copy(attn, attn_out, ld_sem.at[4])
    st_attn.start()
    done = CH
    for k in reversed(range(hops - 1)):
        for o in [k, -k] if k else [0]:
            for_sibling(o)
        for o in [k, -k] if k else [0]:
            for_ring(o)
        for n in range(done, min(done + CH, msgs)):
            step(n)
        done = min(done + CH, msgs)
    base = msgs - CH
    stores = []
    for i in turned:
        n_r = base + turned.index(i)
        n_l = base + turned.index(CH - 1 - i)
        value = both(0, i)
        rs_r(n_r).wait_recv()
        rs_l(n_l).wait_recv()
        fin[pl.ds(i * piece, piece), :] = (
            value + rrecv[n_r].astype(F32) + lrecv[n_l].astype(F32)
        )
        stores.append(
            pltpu.make_async_copy(piece_of(fin, i), piece_of(input_grad, i), ld_sem.at[7 + i])
        )
        stores[-1].start()
    for dz in range(1, Z):
        remote(
            bk.at[zat(dz)], sliced(rt, z), pc_s.at[dz - 1], pc_r.at[dz - 1], zpeer(dz)
        ).wait_send()
    for s in range(1, Y):
        rsib(s).wait_send()
    for n in range(CH // 2):
        x_r(n).wait_send()
        x_l(n).wait_send()
    for i in range(msgs):
        rs_r(i).wait_send()
        rs_l(i).wait_send()
    st_attn.wait()
    for cp in stores:
        cp.wait()


def local(X, Z, Y, tokens, w_qkv, forget, out_grad, doc_lengths):
    R, F = tokens.shape
    D, C = w_qkv.shape[1:]
    heads = C // DH
    docs = doc_lengths.shape[0]
    TP = 2 * Y
    hops = Y // 2
    msgs = (hops - 1) * CHUNKS + CHUNKS // 2
    piece = R // CHUNKS
    SR = -(-2 * heads * DH // Z)
    SR = -(-SR // 16) * 16
    dma = pltpu.SemaphoreType.DMA
    V = pltpu.VMEM
    scratch = [
        pltpu.SMEM((docs,), jnp.int32),
        V((3, D, C), BF16), V((TP, R, F), BF16), V((heads, R), F32), V((R, C), BF16),
        V((3, R, C), F32), V((3, R, C), BF16), V((3, R, C), BF16), V((R, C), F32), V((R, C), F32),
        V((heads, R, R), F32), V((heads, R, DH), F32), V((heads, R, DH), F32), V((4, R, C), F32),
        V((8, DH), F32), V((Z, 8, DH), F32), V((8, DH), F32), V((X, 8, DH), F32),
        V((Z, SR, DH), F32), V((Z, SR, DH), F32), V((Z, SR, DH), F32), V((Z, SR, DH), F32),
        V((Z * SR, DH), BF16), V((Z, SR, DH), BF16), V((SR, DH), BF16), V((X, SR, DH), BF16),
        V((Z, SR, DH), BF16), V((Z * SR, DH), BF16),
        V((Y, R, C), BF16), V((Y, R, C), BF16), V((Y, R, C), F32),
        V((msgs, piece, C), BF16), V((msgs, piece, C), BF16),
        V((msgs, piece, C), BF16), V((msgs, piece, C), BF16),
        dma((7 + CHUNKS,)),
        dma((msgs,)), dma((msgs,)), dma((msgs,)), dma((msgs,)),
        dma((2 * msgs + 1,)), dma((2 * msgs + 1,)),
        dma((Z - 1,)), dma((Z - 1,)), dma((X - 1,)), dma((X - 1,)),
        dma((Z - 1,)), dma((Z - 1,)), dma((X - 1,)), dma((X - 1,)),
        dma((Z - 1,)), dma((Z - 1,)),
        dma((Y,)), dma((Y,)), dma((msgs,)), dma((msgs,)), dma((msgs,)), dma((msgs,)),
        V((CHUNKS // 2, piece, C), BF16), V((CHUNKS // 2, piece, C), BF16),
        dma((CHUNKS // 2,)), dma((CHUNKS // 2,)), dma((CHUNKS // 2,)), dma((CHUNKS // 2,)),
    ]
    anywhere = pl.BlockSpec(memory_space=pltpu.HBM)
    return pl.pallas_call(
        functools.partial(kernel, X, Z, Y, R, C, SR, docs),
        out_shape=(
            jax.ShapeDtypeStruct((R, C), F32),
            jax.ShapeDtypeStruct((R, F), F32),
        ),
        in_specs=[anywhere] * 5,
        out_specs=(anywhere, anywhere),
        scratch_shapes=scratch,
        compiler_params=pltpu.CompilerParams(
            collective_id=0, has_side_effects=True, vmem_limit_bytes=64 * 1024 * 1024
        ),
        name="decayed_attention_step",
    )(tokens, w_qkv, forget.T, out_grad, doc_lengths)


X_CHIPS = 4


def solution(mesh, x_chips=X_CHIPS):
    seq, tp = mesh.shape["seq"], mesh.shape["tp"]
    placed = (P("seq", "tp"), P(None, None, "tp"), P("seq", "tp"), P("seq", "tp"), P())
    return jax.shard_map(
        functools.partial(local, x_chips, seq // x_chips, tp // 2),
        mesh=mesh,
        in_specs=placed,
        out_specs=(P("seq", "tp"), P("seq", "tp")),
        check_vma=False,
    )
```

```python
import functools

import jax
import jax.numpy as jnp
from jax import lax
from jax.experimental import pallas as pl
from jax.experimental.pallas import tpu as pltpu
from jax.sharding import PartitionSpec as P

DH = 128
CHUNKS = 4
F32 = jnp.float32
BF16 = jnp.bfloat16
MESH = pl.DeviceIdType.MESH


def dot_nn(a, b):
    return lax.dot_general(a, b, (((1,), (0,)), ((), ())), preferred_element_type=F32)


def dot_nt(a, b):
    return lax.dot_general(a, b, (((1,), (1,)), ((), ())), preferred_element_type=F32)


def dot_tn(a, b):
    return lax.dot_general(a, b, (((0,), (0,)), ((), ())), preferred_element_type=F32)


def kernel(
    X, Z, Y, R, C, SR, docs,
    tokens, w, forget, out_grad, doc_hbm,
    attn_out, input_grad,
    doc_lengths, wv, tok, fg, og, acc, qkv, gr, attn, fin,
    weight, lead, tail, part,
    lzs, lz, lxs, lx, coef, cum, share_of, pre,
    st, rc, ts, tx, bk, rt,
    sbs, sbr, own, rsend, rrecv, lsend, lrecv,
    ld_sem,
    agr_s, agr_r, agl_s, agl_r, sib_s, sib_r,
    e1_s, e1_r, e2_s, e2_r, pa_s, pa_r, pb_s, pb_r, pc_s, pc_r,
    rsib_s, rsib_r, rsr_s, rsr_r, rsl_s, rsl_r,
    xr, xl, xr_s, xr_r, xl_s, xl_r,
):
    heads = C // DH
    CH = CHUNKS
    piece = R // CH
    hops = Y // 2
    msgs = (hops - 1) * CH + CH // 2
    seq = lax.axis_index("seq")
    tp = lax.axis_index("tp")
    x = lax.div(seq, Z)
    z = lax.rem(seq, Z)
    y = lax.div(tp, 2)
    c = lax.rem(tp, 2)

    def chip(o):
        return lax.rem(y + (o + Y), Y)

    right = (seq, chip(1) * 2 + c)
    left = (seq, chip(-1) * 2 + c)
    sibling = (seq, y * 2 + (1 - c))
    right_x = (seq, chip(1) * 2 + (1 - c))
    left_x = (seq, chip(-1) * 2 + (1 - c))

    def zat(dz):
        return lax.rem(z + dz, Z)

    def xat(dx):
        return lax.rem(x + dx, X)

    def zpeer(dz):
        return (x * Z + zat(dz), tp)

    def xpeer(dx):
        return (xat(dx) * Z + z, tp)

    def remote(src, dst, ssem, rsem, dev):
        return pltpu.make_async_remote_copy(
            src_ref=src, dst_ref=dst, send_sem=ssem, recv_sem=rsem,
            device_id=dev, device_id_type=MESH,
        )

    own_tok = tok.at[tp]
    ld_tok = pltpu.make_async_copy(tokens, own_tok, ld_sem.at[0])
    ld_fg = pltpu.make_async_copy(forget, fg, ld_sem.at[1])
    ld_w = pltpu.make_async_copy(w, wv, ld_sem.at[2])
    ld_og = pltpu.make_async_copy(out_grad, og, ld_sem.at[3])
    ld_tok.start()
    ld_fg.start()
    ld_w.start()
    ld_og.start()
    ld_doc = pltpu.make_async_copy(doc_hbm, doc_lengths, ld_sem.at[6])
    ld_doc.start()

    barrier = pltpu.get_barrier_semaphore()
    peers = [right, left, sibling, right_x, left_x]
    peers += [zpeer(dz) for dz in range(1, Z)]
    peers += [xpeer(dx) for dx in range(1, X)]
    for dev in peers:
        pl.semaphore_signal(barrier, inc=1, device_id=dev, device_id_type=MESH)
    pl.semaphore_wait(barrier, len(peers))

    def piece_of(ref, i):
        return ref.at[pl.ds(i * piece, piece)]

    def r_place(i, shift):
        return piece_of(tok.at[chip(-(i // CH) - shift) * 2 + c], i % CH)

    def l_place(i, shift):
        return piece_of(tok.at[chip(i // CH + shift) * 2 + c], CH - 1 - i % CH)

    def r_source(i):
        return piece_of(tokens, i) if i < CH else r_place(i, 0)

    def l_source(i):
        return piece_of(tokens, CH - 1 - i) if i < CH else l_place(i, 0)

    ag_r = [remote(r_source(i), r_place(i, 0), agr_s.at[i], agr_r.at[i], right) for i in range(msgs)]
    ag_l = [remote(l_source(i), l_place(i, 0), agl_s.at[i], agl_r.at[i], left) for i in range(msgs)]
    in_r = [remote(r_place(i, 1), r_place(i, 1), agr_s.at[i], agr_r.at[i], right) for i in range(msgs)]
    in_l = [remote(l_place(i, 1), l_place(i, 1), agl_s.at[i], agl_r.at[i], left) for i in range(msgs)]

    def sib_place(k, core):
        if k == 0:
            return tok.at[y * 2 + core]
        if k <= msgs:
            i = k - 1
            return piece_of(tok.at[chip(-(i // CH) - 1) * 2 + core], i % CH)
        i = k - 1 - msgs
        return piece_of(tok.at[chip(i // CH + 1) * 2 + core], CH - 1 - i % CH)

    sib_out = [
        remote(sib_place(k, c) if k else tokens, sib_place(k, c), sib_s.at[k], sib_r.at[k], sibling)
        for k in range(2 * msgs + 1)
    ]
    last_hop = (hops - 1) * CH
    for i in range(last_hop, msgs):
        k = 1 + i
        sib_out[k] = remote(r_place(i, 0), r_place(i, 0), sib_s.at[k], sib_r.at[k], right_x)
        k = 1 + msgs + i
        sib_out[k] = remote(l_place(i, 0), l_place(i, 0), sib_s.at[k], sib_r.at[k], left_x)
    sib_in = [
        remote(sib_place(k, 1 - c), sib_place(k, 1 - c), sib_s.at[k], sib_r.at[k], sibling)
        for k in range(2 * msgs + 1)
    ]

    for i in range(CH):
        ag_r[i].start()
        ag_l[i].start()
    sib_out[0].start()

    near = sorted(range(1, Z), key=lambda dz: -min(dz, Z - dz))
    across = sorted(range(1, X), key=lambda dx: -min(dx, X - dx))
    ld_fg.wait()
    rows = lax.broadcasted_iota(jnp.int32, (R, R), 0)
    cols = lax.broadcasted_iota(jnp.int32, (R, R), 1)
    sums = []
    for h in range(heads):
        frow = jnp.broadcast_to(fg[h : h + 1, :], (R, R))
        lcol = jnp.sum(jnp.where(cols <= rows, frow, 0.0), axis=1, keepdims=True)
        lrow = jnp.sum(jnp.where(rows == cols, lcol, 0.0), axis=0, keepdims=True)
        sums.append((lcol, lrow, lrow[:, R - 1 : R]))
    row8 = lax.broadcasted_iota(jnp.int32, (8, DH), 0)
    lzs[...] = jnp.where(row8 == 0, sums[0][2], sums[1][2])
    e1 = [remote(lzs, lz.at[z], e1_s.at[dz - 1], e1_r.at[dz - 1], zpeer(dz)) for dz in near]
    for cp in e1:
        cp.start()
    lz[z] = lzs[...]

    ld_doc.wait()
    ends = []
    total = jnp.int32(0)
    for j in range(docs):
        total = total + doc_lengths[j]
        ends.append(total)
    offset = seq * R

    def doc_of(position):
        count = jnp.int32(0)
        for e in ends:
            count = count + jnp.where(position >= e, 1, 0).astype(jnp.int32)
        return count

    def weights():
        prior = jnp.where(offset > 0, doc_of(offset - 1), -1)
        last = doc_of(offset + R - 1)
        doc_row = doc_of(offset + lax.broadcasted_iota(jnp.int32, (1, R), 1))
        doc_col = doc_of(offset + lax.broadcasted_iota(jnp.int32, (R, 1), 0))
        mask = (doc_col == doc_row) & (rows >= cols)
        lane = (R, DH)
        for h in range(heads):
            lcol, lrow, ltot = sums[h]
            gap = jnp.where(mask, lcol - lrow, 0.0)
            weight[h] = jnp.where(mask, jnp.exp(gap), 0.0)
            lead[h] = jnp.broadcast_to(jnp.where(doc_col == prior, jnp.exp(lcol), 0.0), lane)
            tail[h] = jnp.broadcast_to(
                jnp.where(doc_col == last, jnp.exp(ltot - lcol), 0.0), lane
            )

    srow = lax.broadcasted_iota(jnp.int32, (SR, DH), 0) + z * SR
    is_back = srow >= heads * DH
    second = (lax.rem(srow, 2 * DH)) >= DH

    def decays():
        for dz in range(1, Z):
            src = lax.rem(z + (Z - dz), Z)
            remote(lzs, lz.at[src], e1_s.at[dz - 1], e1_r.at[dz - 1], zpeer(dz)).wait_recv()
        place = x * Z + lax.broadcasted_iota(jnp.int32, (16, DH), 0)
        through = place > 0
        for e in ends:
            through = through & jnp.logical_not((e >= place * R) & (e < place * R + R))
        thru = jnp.where(through, 1.0, 0.0)
        a = []
        for p in range(Z):
            v = lz[p]
            a.append([jnp.where(thru[p : p + 1] > 0, jnp.exp(v[h : h + 1]), 0.0) for h in range(heads)])
        up = [jnp.ones((1, DH), F32)] * heads
        for p in range(Z):
            coef[p] = jnp.where(second, a[p][1], a[p][0])
            cum[p] = jnp.where(second, up[1], up[0])
            share_of[p] = cum[p]
            up = [up[h] * a[p][h] for h in range(heads)]
        down = [jnp.ones((1, DH), F32)] * heads
        for p in reversed(range(Z)):
            below = jnp.where(second, down[1], down[0])
            share_of[p] = jnp.where(is_back, share_of[p], below)
            cum[p] = jnp.where(is_back, below, cum[p])
            down = [down[h] * a[p][h] for h in range(heads)]
        lxs[...] = jnp.where(row8 == 0, up[0], up[1])
        lx[x] = lxs[...]
        for dx in across:
            remote(lxs, lx.at[x], e2_s.at[dx - 1], e2_r.at[dx - 1], xpeer(dx)).start()

    def block_term(j, m):
        return dot_nn(tok[j], wv[m, pl.ds(pl.multiple_of(j * C, C), C), :])

    def project_hop(k):
        for m in range(3):
            out = None
            for o in [0] if k == 0 else [-k, k]:
                for core in range(2):
                    term = block_term(chip(o) * 2 + core, m)
                    out = term if out is None else out + term
            acc[m] = out if k == 0 else acc[m] + out

    def sib_wait(k):
        if k == 0:
            sib_in[0].wait_recv()
            return
        for i in range((k - 1) * CH, min(k * CH, msgs)):
            sib_in[1 + i].wait_recv()
            sib_in[1 + msgs + i].wait_recv()

    for k in range(1, hops + 1):
        for i in range((k - 1) * CH, min(k * CH, msgs)):
            in_r[i].wait_recv()
            if i + CH < msgs:
                ag_r[i + CH].start()
            if last_hop <= i + CH < msgs:
                sib_out[1 + i + CH].start()
            if i < last_hop:
                sib_out[1 + i].start()
            in_l[i].wait_recv()
            if i + CH < msgs:
                ag_l[i + CH].start()
            if last_hop <= i + CH < msgs:
                sib_out[1 + msgs + i + CH].start()
            if i < last_hop:
                sib_out[1 + msgs + i].start()
        if k == 1:
            weights()
            ld_tok.wait()
            ld_w.wait()
            ld_og.wait()
        if k == hops - 1:
            decays()
        sib_wait(k - 1)
        project_hop(k - 1)

    far = chip(hops) * 2
    for m in (1, 2, 0):
        acc[m] += block_term(far + c, m)
    sib_wait(hops)
    for m in (1, 2, 0):
        qkv[m] = (acc[m] + block_term(far + 1 - c, m)).astype(BF16)

    def head(m, h):
        return qkv[m, :, pl.ds(h * DH, DH)]

    def grad_head(h):
        return og[:, pl.ds(h * DH, DH)]

    def two_terms(value):
        high = value.astype(BF16)
        return high, (value - high.astype(F32)).astype(BF16)

    for h in range(heads):
        kt, kt2 = two_terms(head(1, h).astype(F32) * tail[h])
        state = dot_tn(kt, head(2, h)) + dot_tn(kt2, head(2, h))
        st[pl.ds(h * DH, DH), :] = state.astype(BF16)
        ql, ql2 = two_terms(head(0, h).astype(F32) * lead[h])
        st[pl.ds((heads + h) * DH, DH), :] = (
            (dot_tn(ql, grad_head(h)) + dot_tn(ql2, grad_head(h))) * (1.0 / DH)
        ).astype(BF16)
    if Z * SR > 2 * heads * DH:
        spare = Z * SR - 2 * heads * DH
        st[pl.ds(2 * heads * DH, spare), :] = jnp.zeros((spare, DH), BF16)

    def sliced(ref, p):
        return ref.at[pl.ds(pl.multiple_of(p * SR, SR), SR)]

    for dz in near:
        remote(
            sliced(st, zat(dz)), rc.at[z], pa_s.at[dz - 1], pa_r.at[dz - 1], zpeer(dz)
        ).start()
    rc[z] = st[pl.ds(pl.multiple_of(z * SR, SR), SR), :]

    def inside(h):
        q, k, v, g = head(0, h), head(1, h), head(2, h), grad_head(h)
        cols_h = pl.ds(h * DH, DH)
        a, a2 = two_terms(dot_nt(q, k) * weight[h])
        b, b2 = two_terms(dot_nt(g, v) * weight[h])
        part[0, :, cols_h] = dot_nn(a, v) + dot_nn(a2, v)
        part[1, :, cols_h] = dot_nn(b, k) + dot_nn(b2, k)
        part[2, :, cols_h] = dot_tn(b, q) + dot_tn(b2, q)
        part[3, :, cols_h] = dot_tn(a, g) + dot_tn(a2, g)

    for h in range(heads):
        inside(h)

    for dz in range(1, Z):
        src = lax.rem(z + (Z - dz), Z)
        remote(
            sliced(st, src), rc.at[src], pa_s.at[dz - 1], pa_r.at[dz - 1], zpeer(dz)
        ).wait_recv()
    line_total = share_of[0] * rc[0].astype(F32)
    for p in range(1, Z):
        line_total = line_total + share_of[p] * rc[p].astype(F32)
    ts[...] = line_total.astype(BF16)
    for dx in across:
        remote(ts, tx.at[x], pb_s.at[dx - 1], pb_r.at[dx - 1], xpeer(dx)).start()
    tx[x] = ts[...]

    run = jnp.zeros((SR, DH), F32)
    for p in range(Z):
        pre[p] = run
        run = coef[p] * run + rc[p].astype(F32)
    back = jnp.zeros((SR, DH), F32)
    for p in reversed(range(Z)):
        pre[p] = jnp.where(is_back, back, pre[p])
        back = coef[p] * back + rc[p].astype(F32)

    for dx in range(1, X):
        src = lax.rem(x + (X - dx), X)
        remote(lxs, lx.at[src], e2_s.at[dx - 1], e2_r.at[dx - 1], xpeer(dx)).wait_recv()
        remote(ts, tx.at[src], pb_s.at[dx - 1], pb_r.at[dx - 1], xpeer(dx)).wait_recv()
    run = jnp.zeros((SR, DH), F32)
    back = jnp.zeros((SR, DH), F32)
    for p in range(X):
        v = lx[p]
        line = jnp.where(second, v[1:2], v[0:1])
        run = jnp.where(x > p, line * run + tx[p].astype(F32), run)
    for p in reversed(range(X)):
        v = lx[p]
        line = jnp.where(second, v[1:2], v[0:1])
        back = jnp.where(x < p, line * back + tx[p].astype(F32), back)
    carry = jnp.where(is_back, back, run)

    def entering(p):
        bk[p] = (pre[p] + cum[p] * carry).astype(BF16)

    for dz in near:
        entering(zat(dz))
        remote(
            bk.at[zat(dz)], sliced(rt, z), pc_s.at[dz - 1], pc_r.at[dz - 1], zpeer(dz)
        ).start()
    entering(z)
    rt[pl.ds(pl.multiple_of(z * SR, SR), SR), :] = bk[z]

    for cp in ag_r + ag_l + sib_out + e1:
        cp.wait_send()
    for dx in range(1, X):
        remote(lxs, lx.at[x], e2_s.at[dx - 1], e2_r.at[dx - 1], xpeer(dx)).wait_send()
        remote(ts, tx.at[x], pb_s.at[dx - 1], pb_r.at[dx - 1], xpeer(dx)).wait_send()
    for dz in near:
        remote(
            sliced(st, zat(dz)), rc.at[z], pa_s.at[dz - 1], pa_r.at[dz - 1], zpeer(dz)
        ).wait_send()

    for dz in range(1, Z):
        src = lax.rem(z + (Z - dz), Z)
        remote(
            bk.at[src], sliced(rt, src), pc_s.at[dz - 1], pc_r.at[dz - 1], zpeer(dz)
        ).wait_recv()

    scale = 1.0 / DH
    for h in range(heads):
        k, v, g = head(1, h), head(2, h), grad_head(h)
        cols_h = pl.ds(h * DH, DH)
        state = rt[pl.ds(h * DH, DH), :]
        after = rt[pl.ds((heads + h) * DH, DH), :]
        gr[0, :, cols_h] = (
            (part[1, :, cols_h] + lead[h] * dot_nt(g, state)) * scale
        ).astype(BF16)
        gr[1, :, cols_h] = (
            part[2, :, cols_h] * scale + tail[h] * dot_nt(v, after)
        ).astype(BF16)
        gr[2, :, cols_h] = (
            part[3, :, cols_h] * scale + tail[h] * dot_nn(k, after)
        ).astype(BF16)

    order = [hops]
    for k in reversed(range(1, hops)):
        order += [k, -k]
    order.append(0)
    slot = {o: i for i, o in enumerate(order)}
    slot[-hops] = slot[hops]

    def share(j):
        out = None
        for m in range(3):
            term = dot_nt(gr[m], wv[m, pl.ds(pl.multiple_of(j * C, C), C), :])
            out = term if out is None else out + term
        return out

    def rsib(s):
        return remote(sbs.at[s], sbr.at[s], rsib_s.at[s], rsib_r.at[s], sibling)

    def x_r(n):
        return remote(piece_of(sbs.at[0], n), xr.at[n], xr_s.at[n], xr_r.at[n], right_x)

    def x_l(n):
        return remote(piece_of(sbs.at[0], CH - 1 - n), xl.at[n], xl_s.at[n], xl_r.at[n], left_x)

    def for_sibling(o):
        sbs[slot[o]] = share(chip(o) * 2 + (1 - c)).astype(BF16)
        rsib(slot[o]).start()

    def for_ring(o):
        own[slot[o]] = share(chip(o) * 2 + c)

    joined = set()

    def both(o, i):
        s = slot[o]
        if s == 0:
            return own[s, pl.ds(i * piece, piece), :]
        if s not in joined:
            rsib(s).wait_recv()
            joined.add(s)
        part_rows = pl.ds(i * piece, piece)
        return own[s, part_rows, :] + sbr[s, part_rows, :].astype(F32)

    def rs_r(i):
        return remote(rsend.at[i], rrecv.at[i], rsr_s.at[i], rsr_r.at[i], right)

    def rs_l(i):
        return remote(lsend.at[i], lrecv.at[i], rsl_s.at[i], rsl_r.at[i], left)

    ring = [(hops, i) for i in range(CH // 2)]
    turned = [*range(CH // 2, CH), *range(CH // 2)]
    for k in reversed(range(1, hops)):
        ring += [(k, i) for i in turned]

    def step(n):
        o, i = ring[n]
        value = both(o, i)
        if n >= CH:
            rs_r(n - CH).wait_recv()
            value = value + rrecv[n - CH].astype(F32)
            if n - CH < CH // 2:
                x_r(n - CH).wait_recv()
                value = value + xr[n - CH].astype(F32)
        rsend[n] = value.astype(BF16)
        rs_r(n).start()
        value = both(-o, CH - 1 - i)
        if n >= CH:
            rs_l(n - CH).wait_recv()
            value = value + lrecv[n - CH].astype(F32)
            if n - CH < CH // 2:
                x_l(n - CH).wait_recv()
                value = value + xl[n - CH].astype(F32)
        lsend[n] = value.astype(BF16)
        rs_l(n).start()

    sbs[0] = share(chip(hops) * 2 + (1 - c)).astype(BF16)
    for n in range(CH // 2):
        x_r(n).start()
        x_l(n).start()
    for_ring(hops)
    for n in range(CH // 2):
        step(n)
    for_sibling(hops - 1)
    for_sibling(1 - hops)
    for_ring(hops - 1)
    for_ring(1 - hops)
    for n in range(CH // 2, CH):
        step(n)
    for h in range(heads):
        cols_h = pl.ds(h * DH, DH)
        state = rt[pl.ds(h * DH, DH), :]
        attn[:, cols_h] = (part[0, :, cols_h] + lead[h] * dot_nn(head(0, h), state)) * scale
    st_attn = pltpu.make_async_copy(attn, attn_out, ld_sem.at[4])
    st_attn.start()
    done = CH
    for k in reversed(range(hops - 1)):
        for o in [k, -k] if k else [0]:
            for_sibling(o)
        for o in [k, -k] if k else [0]:
            for_ring(o)
        for n in range(done, min(done + CH, msgs)):
            step(n)
        done = min(done + CH, msgs)
    base = msgs - CH
    stores = []
    for i in turned:
        n_r = base + turned.index(i)
        n_l = base + turned.index(CH - 1 - i)
        value = both(0, i)
        rs_r(n_r).wait_recv()
        rs_l(n_l).wait_recv()
        fin[pl.ds(i * piece, piece), :] = (
            value + rrecv[n_r].astype(F32) + lrecv[n_l].astype(F32)
        )
        stores.append(
            pltpu.make_async_copy(piece_of(fin, i), piece_of(input_grad, i), ld_sem.at[7 + i])
        )
        stores[-1].start()
    for dz in range(1, Z):
        remote(
            bk.at[zat(dz)], sliced(rt, z), pc_s.at[dz - 1], pc_r.at[dz - 1], zpeer(dz)
        ).wait_send()
    for s in range(1, Y):
        rsib(s).wait_send()
    for n in range(CH // 2):
        x_r(n).wait_send()
        x_l(n).wait_send()
    for i in range(msgs):
        rs_r(i).wait_send()
        rs_l(i).wait_send()
    st_attn.wait()
    for cp in stores:
        cp.wait()


def local(X, Z, Y, tokens, w_qkv, forget, out_grad, doc_lengths):
    R, F = tokens.shape
    D, C = w_qkv.shape[1:]
    heads = C // DH
    docs = doc_lengths.shape[0]
    TP = 2 * Y
    hops = Y // 2
    msgs = (hops - 1) * CHUNKS + CHUNKS // 2
    piece = R // CHUNKS
    SR = -(-2 * heads * DH // Z)
    SR = -(-SR // 16) * 16
    dma = pltpu.SemaphoreType.DMA
    V = pltpu.VMEM
    scratch = [
        pltpu.SMEM((docs,), jnp.int32),
        V((3, D, C), BF16), V((TP, R, F), BF16), V((heads, R), F32), V((R, C), BF16),
        V((3, R, C), F32), V((3, R, C), BF16), V((3, R, C), BF16), V((R, C), F32), V((R, C), F32),
        V((heads, R, R), F32), V((heads, R, DH), F32), V((heads, R, DH), F32), V((4, R, C), F32),
        V((8, DH), F32), V((Z, 8, DH), F32), V((8, DH), F32), V((X, 8, DH), F32),
        V((Z, SR, DH), F32), V((Z, SR, DH), F32), V((Z, SR, DH), F32), V((Z, SR, DH), F32),
        V((Z * SR, DH), BF16), V((Z, SR, DH), BF16), V((SR, DH), BF16), V((X, SR, DH), BF16),
        V((Z, SR, DH), BF16), V((Z * SR, DH), BF16),
        V((Y, R, C), BF16), V((Y, R, C), BF16), V((Y, R, C), F32),
        V((msgs, piece, C), BF16), V((msgs, piece, C), BF16),
        V((msgs, piece, C), BF16), V((msgs, piece, C), BF16),
        dma((7 + CHUNKS,)),
        dma((msgs,)), dma((msgs,)), dma((msgs,)), dma((msgs,)),
        dma((2 * msgs + 1,)), dma((2 * msgs + 1,)),
        dma((Z - 1,)), dma((Z - 1,)), dma((X - 1,)), dma((X - 1,)),
        dma((Z - 1,)), dma((Z - 1,)), dma((X - 1,)), dma((X - 1,)),
        dma((Z - 1,)), dma((Z - 1,)),
        dma((Y,)), dma((Y,)), dma((msgs,)), dma((msgs,)), dma((msgs,)), dma((msgs,)),
        V((CHUNKS // 2, piece, C), BF16), V((CHUNKS // 2, piece, C), BF16),
        dma((CHUNKS // 2,)), dma((CHUNKS // 2,)), dma((CHUNKS // 2,)), dma((CHUNKS // 2,)),
    ]
    anywhere = pl.BlockSpec(memory_space=pltpu.HBM)
    return pl.pallas_call(
        functools.partial(kernel, X, Z, Y, R, C, SR, docs),
        out_shape=(
            jax.ShapeDtypeStruct((R, C), F32),
            jax.ShapeDtypeStruct((R, F), F32),
        ),
        in_specs=[anywhere] * 5,
        out_specs=(anywhere, anywhere),
        scratch_shapes=scratch,
        compiler_params=pltpu.CompilerParams(
            collective_id=0, has_side_effects=True, vmem_limit_bytes=64 * 1024 * 1024
        ),
        name="decayed_attention_step",
    )(tokens, w_qkv, forget.T, out_grad, doc_lengths)


X_CHIPS = 4


def solution(mesh, x_chips=X_CHIPS):
    seq, tp = mesh.shape["seq"], mesh.shape["tp"]
    placed = (P("seq", "tp"), P(None, None, "tp"), P("seq", "tp"), P("seq", "tp"), P())
    return jax.shard_map(
        functools.partial(local, x_chips, seq // x_chips, tp // 2),
        mesh=mesh,
        in_specs=placed,
        out_specs=(P("seq", "tp"), P("seq", "tp")),
        check_vma=False,
    )
```
